32 devices in a mesh: prow: 4 (over y, x), pcol: 8 (over z, core).
Axes of the slice: x: 2, y: 2, z: 4, core: 2. Of those that a mesh axis runs over, the one named last changes fastest.
Arguments:
- matrix: float32 [2048, 1024], P('prow', 'pcol'), may hold values from -6 to 6
- panel: float32 [2048, 1024], P(('prow', 'pcol')), as said below
- pivots: int32 [1024], replicated, may hold values from 0 to 2047, as said below
Outputs:
- trailing: float32 [2048, 1024], P('prow', 'pcol')
The draws below stay inside these ranges and needn't reach their ends.
Inputs may be any that keep to these rules, and one draw needn't show every extreme that they name: pivots[i] is either i itself or a row at or beyond 1024; the rows at or beyond 1024 that are named are all different; at most 264 of them lie in the rows of one index of prow, and some index of prow holds exactly 264. `panel`: the top 1024 rows are unit lower triangular.
All inputs are finite; a program needn't handle non-finite values.
Results may differ from the reference program's by a relative error of at most 0.000061.
Values sent between devices are 32-bit elements; how exact they have to be, the bound alone decides.
No kernel may reach another device: no remote copies, remote signals or barrier semaphores. Data moves between devices by JAX's collectives and lax.ppermute only.
A program may use at most 64 MiB of HBM per device.

```python
import jax
import jax.numpy as jnp
from jax import lax

NB = 1024
ROWS_DEV = 512
NROWS = 2048
NCOLS = 1024
CAP = 264


def draw_pivots(key, part):
    sources = NB // ROWS_DEV
    count = NROWS // ROWS_DEV - sources
    moved_total = NB // 2
    local = jax.vmap(lambda sub: jax.random.permutation(sub, ROWS_DEV))(jax.random.split(jax.random.fold_in(key, 31), count))
    last_perm = local[count - 1]
    where_last = jnp.argmax(last_perm == ROWS_DEV - 1)
    swapped = last_perm.at[where_last].set(last_perm[0]).at[0].set(ROWS_DEV - 1)
    local = local.at[count - 1].set(swapped)
    candidates = (jnp.arange(count)[:, None] + sources) * ROWS_DEV + local[:, :CAP]
    planted = jax.random.randint(jax.random.fold_in(key, 32), (), 0, count)
    order_score = jax.random.permutation(jax.random.fold_in(key, 33), count)
    devices = jnp.arange(count)
    score = jnp.where(devices == planted, -2, jnp.where(devices == count - 1, -1, order_score))
    device_order = jnp.argsort(score)
    flat = candidates[device_order].reshape(-1)
    ranking = jax.random.permutation(jax.random.fold_in(key, 34), NB)
    targets = flat[jnp.minimum(ranking, count * CAP - 1)]
    return jnp.where(ranking < moved_total, targets, jnp.arange(NB)).astype(jnp.int32)


def draw_panel(key, part):
    base = jax.random.normal(jax.random.fold_in(key, 21), (NROWS, NB), jnp.float32)
    base = base / NB ** 0.5
    row_ids = jnp.arange(NROWS)[:, None]
    col_ids = jnp.arange(NB)[None, :]
    lower_tri = jnp.where(col_ids < row_ids, base, 0.0) + jnp.where(col_ids == row_ids, 1.0, 0.0)
    return jnp.where(row_ids < NB, lower_tri, base).astype(jnp.float32)


def shard_levels(own_key, dims, shards, low, top_value):
    factor_of = 1.0
    for position, shards_of in shards:
        steps = jax.random.uniform(jax.random.fold_in(jax.random.fold_in(own_key, 6), position), (shards_of,), jnp.float32, low / len(shards), top_value / len(shards))
        factor_of = factor_of * jnp.repeat(jnp.exp(steps), dims[position] // shards_of).reshape((-1,) + (1,) * (len(dims) - 1 - position))
    return factor_of


def centred(rng, shape, width, bound, shards=(), held_as=jnp.bfloat16):
    values = width * jax.random.normal(rng, shape, jnp.float32)
    if shards:
        values = values * shard_levels(rng, shape, shards, -0.22, 0.18)
    return jnp.clip(values, -bound, bound).astype(held_as)


def setup_inputs(seed: int = 0) -> dict:
    key_of = jax.random.split(jax.random.key(seed), 4)
    matrix = centred(key_of[0], (NROWS, NCOLS), 1.0, 6.0, ((0, 4), (1, 8)), jnp.float32)
    panel = draw_panel(jax.random.fold_in(key_of[3], 71), 0)
    pivots = draw_pivots(jax.random.fold_in(key_of[3], 71), 0)
    return {"matrix": matrix, "panel": panel, "pivots": pivots}


def reference(matrix, panel, pivots):
    total = matrix.shape[0]
    block = pivots.shape[0]
    order = jnp.arange(total, dtype=jnp.int32)
    order = order.at[:block].set(pivots.astype(jnp.int32))
    target = jnp.where(pivots >= block, pivots, total).astype(jnp.int32)
    order = order.at[target].set(jnp.arange(block, dtype=jnp.int32), mode="drop")
    permuted = jnp.take(matrix, order, axis=0)
    upper = jnp.dot(panel[:block], permuted[:block], precision=lax.Precision.HIGHEST, preferred_element_type=jnp.float32)
    lower = permuted[block:] - jnp.dot(panel[block:], upper, precision=lax.Precision.HIGHEST, preferred_element_type=jnp.float32)
    return jnp.concatenate([upper, lower], axis=0)
```

```python
import functools

import jax
import jax.numpy as jnp
from jax import lax
from jax.experimental import pallas as pl
from jax.experimental.pallas import tpu as pltpu
from jax.sharding import PartitionSpec as P


VMEM = pl.BlockSpec(memory_space=pltpu.VMEM)
SMEM = pl.BlockSpec(memory_space=pltpu.SMEM)


def swap(block, axis, mask):
    return lax.ppermute(block, axis, [(i, i ^ mask) for i in range(lax.axis_size(axis))])


def halves(value):
    high = value.astype(jnp.bfloat16)
    return high, (value - high.astype(jnp.float32)).astype(jnp.bfloat16)


def dot(a, b):
    return lax.dot_general(a, b, (((1,), (0,)), ((), ())), preferred_element_type=jnp.float32)


def prepare(n_rows, sources, where_ref, piv_row, piv_col, *refs):
    *blocks, top_ref, own_ref, whole = refs
    rows, cols = blocks[0].shape
    block = piv_row.shape[1]
    me = where_ref[0]
    for mask, ref in enumerate(blocks):
        whole[pl.ds(pl.multiple_of((me ^ mask) * rows, rows), rows), :] = ref[...]

    @pl.when(me < sources)
    def _():
        pivot = piv_col[...]
        high, low = halves(whole[pl.ds(0, block), :])
        picked = jnp.concatenate([high.astype(jnp.float32), low.astype(jnp.float32)], axis=1)
        picked = jnp.where(pivot < block, picked, 0.0)
        for source in range(sources, n_rows):
            ids = lax.broadcasted_iota(jnp.int32, (block, rows), 1) + source * rows
            chosen = (pivot == ids).astype(jnp.float32).astype(jnp.bfloat16)
            pair = jnp.concatenate(halves(whole[pl.ds(source * rows, rows), :]), axis=1)
            picked = picked + dot(chosen, pair)
        top_ref[...] = picked.astype(jnp.bfloat16)

    @pl.when(me >= sources)
    def _():
        ids = lax.broadcasted_iota(jnp.int32, (rows, block), 0) + me * rows
        match = piv_row[...] == ids
        chosen = match.astype(jnp.float32)
        named = jnp.max(chosen, axis=1, keepdims=True) > 0.0
        old = whole[pl.ds(0, block), :]
        high, middle = halves(old)
        low = (old - high.astype(jnp.float32) - middle.astype(jnp.float32)).astype(jnp.bfloat16)
        terms = dot(chosen.astype(jnp.bfloat16), jnp.concatenate([high, middle, low], axis=1))
        replaced = terms[:, :cols] + terms[:, cols : 2 * cols] + terms[:, 2 * cols :]
        own_ref[...] = jnp.where(named, replaced, blocks[0][...])


def gathered(where_ref, pieces, high, low):
    me = where_ref[1]
    depth = pieces[0].shape[0]
    for mask, ref in enumerate(pieces):
        at = pl.ds(pl.multiple_of((me ^ mask) * depth, depth), depth)
        high[at, :], low[at, :] = halves(ref[...])


def product(high, low, pair):
    cols = pair.shape[1] // 2
    both = dot(high[...], pair)
    return both[:, :cols] + (both[:, cols:] + dot(low[...], pair[:, :cols]))


def solve(sources, where_ref, top_ref, *refs):
    *pieces, out_ref, high, low = refs

    @pl.when(where_ref[0] < sources)
    def _():
        gathered(where_ref, pieces, high, low)
        out_ref[...] = product(high, low, top_ref[...])


def update(sources, masks, where_ref, own_ref, solved_ref, *refs):
    got = refs[: len(masks)]
    *pieces, out_ref, high, low, upper = refs[len(masks) :]
    rows = own_ref.shape[0]
    me = where_ref[0]

    @pl.when(me < sources)
    def _():
        out_ref[...] = solved_ref[...]

    @pl.when(me >= sources)
    def _():
        gathered(where_ref, pieces, high, low)
        for mask, ref in zip(masks, got):
            source = me ^ mask

            @pl.when(source < sources)
            def _():
                upper[pl.ds(pl.multiple_of(source * rows, rows), rows), :] = ref[...]

        pair = jnp.concatenate(halves(upper[...]), axis=1)
        out_ref[...] = own_ref[...] - product(high, low, pair)


def per_device(matrix, panel, pivots):
    rows, cols = matrix.shape
    block = pivots.shape[0]
    n_rows, n_cols = lax.axis_size("prow"), lax.axis_size("pcol")
    sources = block // rows
    where = jnp.stack([lax.axis_index("prow"), lax.axis_index("pcol")]).astype(jnp.int32)

    far = [panel] + [swap(panel, "pcol", mask) for mask in range(2, n_cols, 2)]
    blocks = [matrix] + [swap(matrix, "prow", mask) for mask in range(1, n_rows)]
    pieces = []
    for piece in far:
        pieces += [piece, swap(piece, "pcol", 1)]

    top, own = pl.pallas_call(
        functools.partial(prepare, n_rows, sources),
        out_shape=(
            jax.ShapeDtypeStruct((block, 2 * cols), jnp.bfloat16),
            jax.ShapeDtypeStruct((rows, cols), jnp.float32),
        ),
        in_specs=[SMEM] + [VMEM] * (2 + n_rows),
        out_specs=(VMEM, VMEM),
        scratch_shapes=[pltpu.VMEM((n_rows * rows, cols), jnp.float32)],
        name="prepare",
    )(where, pivots.reshape(1, block), pivots.reshape(block, 1), *blocks)

    split = [pltpu.VMEM((rows, block), jnp.bfloat16)] * 2
    solved = pl.pallas_call(
        functools.partial(solve, sources),
        out_shape=jax.ShapeDtypeStruct((rows, cols), jnp.float32),
        in_specs=[SMEM] + [VMEM] * (1 + n_cols),
        out_specs=VMEM,
        scratch_shapes=split,
        name="solve",
    )(where, top, *pieces)

    masks = tuple(range(sources, n_rows))
    got = [swap(solved, "prow", mask) for mask in masks]
    return pl.pallas_call(
        functools.partial(update, sources, masks),
        out_shape=jax.ShapeDtypeStruct((rows, cols), jnp.float32),
        in_specs=[SMEM] + [VMEM] * (2 + len(masks) + n_cols),
        out_specs=VMEM,
        scratch_shapes=split + [pltpu.VMEM((block, cols), jnp.float32)],
        name="update",
    )(where, own, solved, *got, *pieces)


def solution(mesh):
    placed = (P("prow", "pcol"), P(("prow", "pcol"), None), P())
    return jax.shard_map(
        per_device, mesh=mesh, in_specs=placed, out_specs=P("prow", "pcol"), check_vma=False
    )
```

```python
import functools

import jax
import jax.numpy as jnp
from jax import lax
from jax.experimental import pallas as pl
from jax.experimental.pallas import tpu as pltpu
from jax.sharding import PartitionSpec as P


VMEM = pl.BlockSpec(memory_space=pltpu.VMEM)
SMEM = pl.BlockSpec(memory_space=pltpu.SMEM)


def swap(block, axis, mask):
    return lax.ppermute(block, axis, [(i, i ^ mask) for i in range(lax.axis_size(axis))])


def call(kernel, out_shape, scratch, where, *args):
    return pl.pallas_call(
        kernel,
        out_shape=out_shape,
        in_specs=[SMEM] + [VMEM] * len(args),
        out_specs=jax.tree.map(lambda _: VMEM, out_shape),
        scratch_shapes=scratch,
    )(where, *args)


def halves(value):
    high = value.astype(jnp.bfloat16)
    return high, (value - high.astype(jnp.float32)).astype(jnp.bfloat16)


def dot(a, b):
    return lax.dot_general(a, b, (((1,), (0,)), ((), ())), preferred_element_type=jnp.float32)


def product(high, low, pair):
    cols = pair.shape[1] // 2
    both = dot(high, pair)
    return both[:, :cols] + (both[:, cols:] + dot(low, pair[:, :cols]))


def prepare(n_rows, sources, where_ref, piv_row, piv_col, *refs):
    *blocks, top_ref, own_ref, whole = refs
    rows, cols = blocks[0].shape
    block = piv_row.shape[1]
    me = where_ref[0]
    for mask, ref in enumerate(blocks):
        whole[pl.ds(pl.multiple_of((me ^ mask) * rows, rows), rows), :] = ref[...]

    @pl.when(me < sources)
    def _():
        pivot = piv_col[...]
        high, low = halves(whole[pl.ds(0, block), :])
        picked = jnp.concatenate([high.astype(jnp.float32), low.astype(jnp.float32)], axis=1)
        picked = jnp.where(pivot < block, picked, 0.0)
        for source in range(sources, n_rows):
            ids = lax.broadcasted_iota(jnp.int32, (block, rows), 1) + source * rows
            chosen = (pivot == ids).astype(jnp.float32).astype(jnp.bfloat16)
            pair = jnp.concatenate(halves(whole[pl.ds(source * rows, rows), :]), axis=1)
            picked = picked + dot(chosen, pair)
        top_ref[...] = picked.astype(jnp.bfloat16)

    @pl.when(me >= sources)
    def _():
        ids = lax.broadcasted_iota(jnp.int32, (rows, block), 0) + me * rows
        match = piv_row[...] == ids
        chosen = match.astype(jnp.float32)
        named = jnp.max(chosen, axis=1, keepdims=True) > 0.0
        old = whole[pl.ds(0, block), :]
        high, middle = halves(old)
        low = (old - high.astype(jnp.float32) - middle.astype(jnp.float32)).astype(jnp.bfloat16)
        terms = dot(chosen.astype(jnp.bfloat16), jnp.concatenate([high, middle, low], axis=1))
        replaced = terms[:, :cols] + terms[:, cols : 2 * cols] + terms[:, 2 * cols :]
        own_ref[...] = jnp.where(named, replaced, blocks[0][...])


def collect(order, unit, chunk, me, pieces, high, low):
    for mask, ref in zip(order, pieces):
        at = pl.ds(pl.multiple_of((me ^ mask) * unit, unit), unit)
        start = 0 if ref.shape[0] == unit else chunk * unit
        high[at, :], low[at, :] = halves(ref[pl.ds(start, unit), :])


def early(order, unit, chunk, where_ref, *refs):
    *pieces, high, low = refs
    collect(order, unit, chunk, where_ref[1], pieces, high, low)


def solve(sources, order, unit, chunk, where_ref, top_ref, early_high, early_low, *refs):
    *pieces, out_ref, high, low = refs
    for mask in range(order[0]):
        at = pl.ds(pl.multiple_of((where_ref[1] ^ mask) * unit, unit), unit)
        high[at, :], low[at, :] = early_high[at, :], early_low[at, :]
    collect(order, unit, chunk, where_ref[1], pieces, high, low)

    @pl.when(where_ref[0] < sources)
    def _():
        out_ref[...] = product(high[...], low[...], top_ref[...])


def update(sources, masks, chunks, n_cols, where_ref, own_ref, *refs):
    solved, refs = refs[:chunks], refs[chunks:]
    split, refs = refs[: 2 * chunks], refs[2 * chunks :]
    *got, out_ref, upper = refs
    rows, _ = own_ref.shape
    depth = rows // n_cols
    unit = depth // chunks
    me = where_ref[0]

    @pl.when(me < sources)
    def _():
        for chunk in range(chunks):
            for i in range(n_cols):
                out_ref[pl.ds(i * depth + chunk * unit, unit), :] = solved[chunk][pl.ds(i * unit, unit), :]

    @pl.when(me >= sources)
    def _():
        for m, mask in enumerate(masks):
            source = me ^ mask

            @pl.when(source < sources)
            def _():
                for chunk in range(chunks):
                    ref = got[chunk * len(masks) + m]
                    for i in range(n_cols):
                        at = pl.multiple_of(source * rows, rows) + (i * depth + chunk * unit)
                        upper[pl.ds(pl.multiple_of(at, unit), unit), :] = ref[pl.ds(i * unit, unit), :]

        pair = jnp.concatenate(halves(upper[...]), axis=1)
        for chunk in range(chunks):
            part = product(split[2 * chunk][...], split[2 * chunk + 1][...], pair)
            for i in range(n_cols):
                at = pl.ds(i * depth + chunk * unit, unit)
                out_ref[at, :] = own_ref[at, :] - part[i * unit : (i + 1) * unit]


def per_device(matrix, panel, pivots):
    rows, cols = matrix.shape
    block = pivots.shape[0]
    depth = panel.shape[0]
    n_rows, n_cols = lax.axis_size("prow"), lax.axis_size("pcol")
    sources = block // rows
    chunks = 2 if depth % 32 == 0 else 1
    unit = depth // chunks
    where = jnp.stack([lax.axis_index("prow"), lax.axis_index("pcol")]).astype(jnp.int32)
    f32, bf16 = jnp.float32, jnp.bfloat16

    near = [panel, swap(panel, "pcol", 2)]
    near = [piece for block_ in near for piece in (block_, swap(block_, "pcol", 1))]
    far = []
    for chunk in range(chunks):
        part = panel[chunk * unit : (chunk + 1) * unit]
        got = [swap(part, "pcol", mask) for mask in range(4, n_cols, 2)]
        far.append([piece for block_ in got for piece in (block_, swap(block_, "pcol", 1))])
    blocks = [matrix] + [swap(matrix, "prow", mask) for mask in range(1, n_rows)]

    top, own = call(
        functools.partial(prepare, n_rows, sources),
        (jax.ShapeDtypeStruct((block, 2 * cols), bf16), jax.ShapeDtypeStruct((rows, cols), f32)),
        [pltpu.VMEM((n_rows * rows, cols), f32)],
        where, pivots.reshape(1, block), pivots.reshape(block, 1), *blocks,
    )

    masks = tuple(range(sources, n_rows))
    solved, split, got = [], [], []
    for chunk in range(chunks):
        terms = [jax.ShapeDtypeStruct((rows // chunks, block), bf16)] * 2
        high, low = call(
            functools.partial(early, range(len(near)), unit, chunk),
            terms,
            [],
            where, *near,
        )
        piece, high, low = call(
            functools.partial(solve, sources, tuple(range(len(near), n_cols)), unit, chunk),
            [jax.ShapeDtypeStruct((rows // chunks, cols), f32)] + terms,
            [],
            where, top, high, low, *far[chunk],
        )
        solved.append(piece)
        split += [high, low]
        got += [swap(piece, "prow", mask) for mask in masks]

    return call(
        functools.partial(update, sources, masks, chunks, n_cols),
        jax.ShapeDtypeStruct((rows, cols), f32),
        [pltpu.VMEM((block, cols), f32)],
        where, own, *solved, *split, *got,
    )


def solution(mesh):
    placed = (P("prow", "pcol"), P(("prow", "pcol"), None), P())
    return jax.shard_map(
        per_device, mesh=mesh, in_specs=placed, out_specs=P("prow", "pcol"), check_vma=False
    )
```

```python
import functools

import jax
import jax.numpy as jnp
from jax import lax
from jax.experimental import pallas as pl
from jax.experimental.pallas import tpu as pltpu
from jax.sharding import PartitionSpec as P


VMEM = pl.BlockSpec(memory_space=pltpu.VMEM)


def swap(block, axis, mask):
    return lax.ppermute(block, axis, [(i, i ^ mask) for i in range(lax.axis_size(axis))])


def call(kernel, out_shape, scratch, *args):
    return pl.pallas_call(
        kernel,
        out_shape=out_shape,
        in_specs=[VMEM] * len(args),
        out_specs=jax.tree.map(lambda _: VMEM, out_shape),
        scratch_shapes=scratch,
        compiler_params=pltpu.CompilerParams(vmem_limit_bytes=16 * 2**20),
    )(*(pltpu.with_memory_space_constraint(arg, pltpu.VMEM) for arg in args))


def halves(value):
    high = value.astype(jnp.bfloat16)
    return high, (value - high.astype(jnp.float32)).astype(jnp.bfloat16)


def dot(a, b):
    return lax.dot_general(a, b, (((1,), (0,)), ((), ())), preferred_element_type=jnp.float32)


def product(high, low, pair):
    cols = pair.shape[1] // 2
    both = dot(high, pair)
    return both[:, :cols] + (both[:, cols:] + dot(low, pair[:, :cols]))


def prepare(n_rows, sources, piv_row, *refs):
    *blocks, top_ref, own_ref, whole = refs
    rows, cols = blocks[0].shape
    block = piv_row.shape[1]
    me = lax.axis_index("prow")
    for mask, ref in enumerate(blocks):
        whole[pl.ds(pl.multiple_of((me ^ mask) * rows, rows), rows), :] = ref[...]

    @pl.when(me < sources)
    def _():
        lanes = 128
        pivot = jnp.broadcast_to(piv_row[...], (lanes, block)).T
        high, low = halves(whole[pl.ds(0, block), :])
        picked = jnp.concatenate([high.astype(jnp.float32), low.astype(jnp.float32)], axis=1)
        picked = jnp.where(pivot[:, :1] < block, picked, 0.0)
        for source in range(sources, n_rows):
            ids = lax.broadcasted_iota(jnp.int32, (block, lanes), 1) + source * rows
            chosen = [(pivot - i == ids).astype(jnp.float32).astype(jnp.bfloat16) for i in range(0, rows, lanes)]
            chosen = jnp.concatenate(chosen, axis=1)
            pair = jnp.concatenate(halves(whole[pl.ds(source * rows, rows), :]), axis=1)
            picked = picked + dot(chosen, pair)
        top_ref[...] = picked.astype(jnp.bfloat16)

    @pl.when(me >= sources)
    def _():
        ids = lax.broadcasted_iota(jnp.int32, (rows, block), 0) + me * rows
        match = piv_row[...] == ids
        chosen = match.astype(jnp.float32)
        named = jnp.max(chosen, axis=1, keepdims=True) > 0.0
        old = whole[pl.ds(0, block), :]
        high, middle = halves(old)
        low = (old - high.astype(jnp.float32) - middle.astype(jnp.float32)).astype(jnp.bfloat16)
        terms = dot(chosen.astype(jnp.bfloat16), jnp.concatenate([high, middle, low], axis=1))
        replaced = terms[:, :cols] + terms[:, cols : 2 * cols] + terms[:, 2 * cols :]
        own_ref[...] = jnp.where(named, replaced, blocks[0][...])


def collect(order, unit, chunk, me, pieces, high, low):
    for mask, ref in zip(order, pieces):
        at = pl.ds(pl.multiple_of((me ^ mask) * unit, unit), unit)
        start = 0 if ref.shape[0] == unit else chunk * unit
        high[at, :], low[at, :] = halves(ref[pl.ds(start, unit), :])


def early(order, unit, chunk, *refs):
    *pieces, high, low = refs
    collect(order, unit, chunk, lax.axis_index("pcol"), pieces, high, low)


def solve(sources, order, unit, chunk, top_ref, early_high, early_low, *refs):
    *pieces, out_ref, high, low = refs
    for mask in range(order[0]):
        at = pl.ds(pl.multiple_of((lax.axis_index("pcol") ^ mask) * unit, unit), unit)
        high[at, :], low[at, :] = early_high[at, :], early_low[at, :]
    collect(order, unit, chunk, lax.axis_index("pcol"), pieces, high, low)

    @pl.when(lax.axis_index("prow") < sources)
    def _():
        out_ref[...] = product(high[...], low[...], top_ref[...])


def update(sources, masks, chunks, n_cols, own_ref, *refs):
    solved, refs = refs[:chunks], refs[chunks:]
    split, refs = refs[: 2 * chunks], refs[2 * chunks :]
    *got, out_ref, upper = refs
    rows, _ = own_ref.shape
    depth = rows // n_cols
    unit = depth // chunks
    me = lax.axis_index("prow")

    @pl.when(me < sources)
    def _():
        for chunk in range(chunks):
            for i in range(n_cols):
                out_ref[pl.ds(i * depth + chunk * unit, unit), :] = solved[chunk][pl.ds(i * unit, unit), :]

    @pl.when(me >= sources)
    def _():
        for m, mask in enumerate(masks):
            source = me ^ mask

            @pl.when(source < sources)
            def _():
                for chunk in range(chunks):
                    ref = got[chunk * len(masks) + m]
                    for i in range(n_cols):
                        at = pl.multiple_of(source * rows, rows) + (i * depth + chunk * unit)
                        upper[pl.ds(pl.multiple_of(at, unit), unit), :] = ref[pl.ds(i * unit, unit), :]

        pair = jnp.concatenate(halves(upper[...]), axis=1)
        for chunk in range(chunks):
            part = product(split[2 * chunk][...], split[2 * chunk + 1][...], pair)
            for i in range(n_cols):
                at = pl.ds(i * depth + chunk * unit, unit)
                out_ref[at, :] = own_ref[at, :] - part[i * unit : (i + 1) * unit]


def per_device(matrix, panel, pivots):
    rows, cols = matrix.shape
    block = pivots.shape[0]
    depth = panel.shape[0]
    n_rows, n_cols = lax.axis_size("prow"), lax.axis_size("pcol")
    sources = block // rows
    chunks = 2 if depth % 32 == 0 else 1
    unit = depth // chunks
    f32, bf16 = jnp.float32, jnp.bfloat16

    near = [panel, swap(panel, "pcol", 2)]
    near = [piece for block_ in near for piece in (block_, swap(block_, "pcol", 1))]
    far = []
    for chunk in range(chunks):
        part = panel[chunk * unit : (chunk + 1) * unit]
        got = [swap(part, "pcol", mask) for mask in range(4, n_cols, 2)]
        far.append([piece for block_ in got for piece in (block_, swap(block_, "pcol", 1))])
    blocks = [matrix] + [swap(matrix, "prow", mask) for mask in range(1, n_rows)]

    top, own = call(
        functools.partial(prepare, n_rows, sources),
        (pltpu.VMEM((block, 2 * cols), bf16), pltpu.VMEM((rows, cols), f32)),
        [pltpu.VMEM((n_rows * rows, cols), f32)],
        pivots.reshape(1, block), *blocks,
    )

    masks = tuple(range(sources, n_rows))
    solved, split, got = [], [], []
    for chunk in range(chunks):
        terms = [pltpu.VMEM((rows // chunks, block), bf16)] * 2
        high, low = call(functools.partial(early, range(len(near)), unit, chunk), terms, [], *near)
        piece, high, low = call(
            functools.partial(solve, sources, tuple(range(len(near), n_cols)), unit, chunk),
            [pltpu.VMEM((rows // chunks, cols), f32)] + terms,
            [],
            top, high, low, *far[chunk],
        )
        solved.append(piece)
        split += [high, low]
        got += [swap(piece, "prow", mask) for mask in masks]

    return call(
        functools.partial(update, sources, masks, chunks, n_cols),
        jax.ShapeDtypeStruct((rows, cols), f32),
        [pltpu.VMEM((block, cols), f32)],
        own, *solved, *split, *got,
    )


def solution(mesh):
    placed = (P("prow", "pcol"), P(("prow", "pcol"), None), P())
    return jax.shard_map(
        per_device, mesh=mesh, in_specs=placed, out_specs=P("prow", "pcol"), check_vma=False
    )
```

```python
import functools

import jax
import jax.numpy as jnp
from jax import lax
from jax.experimental import pallas as pl
from jax.experimental.pallas import tpu as pltpu
from jax.sharding import PartitionSpec as P


VMEM = pl.BlockSpec(memory_space=pltpu.VMEM)


def swap(block, axis, mask, among=None):
    ids = range(lax.axis_size(axis)) if among is None else (among, among ^ mask)
    return lax.ppermute(block, axis, [(i, i ^ mask) for i in ids])


def call(kernel, out_shape, scratch, *args):
    return pl.pallas_call(
        kernel,
        out_shape=out_shape,
        in_specs=[VMEM] * len(args),
        out_specs=jax.tree.map(lambda _: VMEM, out_shape),
        scratch_shapes=scratch,
        compiler_params=pltpu.CompilerParams(vmem_limit_bytes=16 * 2**20),
    )(*(pltpu.with_memory_space_constraint(arg, pltpu.VMEM) for arg in args))


def halves(value):
    high = value.astype(jnp.bfloat16)
    return high, (value - high.astype(jnp.float32)).astype(jnp.bfloat16)


def dot(a, b):
    return lax.dot_general(a, b, (((1,), (0,)), ((), ())), preferred_element_type=jnp.float32)


def product(high, low, pair):
    cols = pair.shape[1] // 2
    both = dot(high, pair)
    return both[:, :cols] + (both[:, cols:] + dot(low, pair[:, :cols]))


def halve(rows, panel_ref, first_ref, rest_ref, whole_ref):
    unit = first_ref.shape[0]
    first_ref[...] = panel_ref[pl.ds(0, unit), :]

    @pl.when(lax.axis_index("prow") == 0)
    def _():
        first_ref[:, pl.ds(rows, rows)] = panel_ref[pl.ds(unit, unit), pl.ds(0, rows)]

    rest_ref[...] = panel_ref[pl.ds(unit, unit), :]
    whole_ref[pl.ds(0, unit), :] = first_ref[...]
    whole_ref[pl.ds(unit, unit), :] = rest_ref[...]


def prepare(n_rows, sources, piv_row, *refs):
    *blocks, top_ref, own_ref, whole = refs
    rows, cols = blocks[0].shape
    block = piv_row.shape[1]
    me = lax.axis_index("prow")
    for mask, ref in enumerate(blocks):
        whole[pl.ds(pl.multiple_of((me ^ mask) * rows, rows), rows), :] = ref[...]

    @pl.when(me < sources)
    def _():
        lanes = 128
        pivot = jnp.broadcast_to(piv_row[...], (lanes, block)).T
        high, low = halves(whole[pl.ds(0, block), :])
        picked = jnp.concatenate([high.astype(jnp.float32), low.astype(jnp.float32)], axis=1)
        picked = jnp.where(pivot[:, :1] < block, picked, 0.0)
        for source in range(sources, n_rows):
            ids = lax.broadcasted_iota(jnp.int32, (block, lanes), 1) + source * rows
            chosen = [(pivot - i == ids).astype(jnp.float32).astype(jnp.bfloat16) for i in range(0, rows, lanes)]
            chosen = jnp.concatenate(chosen, axis=1)
            pair = jnp.concatenate(halves(whole[pl.ds(source * rows, rows), :]), axis=1)
            picked = picked + dot(chosen, pair)
        top_ref[...] = picked.astype(jnp.bfloat16)

    @pl.when(me >= sources)
    def _():
        ids = lax.broadcasted_iota(jnp.int32, (rows, block), 0) + me * rows
        match = piv_row[...] == ids
        chosen = match.astype(jnp.float32)
        named = jnp.max(chosen, axis=1, keepdims=True) > 0.0
        old = whole[pl.ds(0, block), :]
        high, middle = halves(old)
        low = (old - high.astype(jnp.float32) - middle.astype(jnp.float32)).astype(jnp.bfloat16)
        terms = dot(chosen.astype(jnp.bfloat16), jnp.concatenate([high, middle, low], axis=1))
        replaced = terms[:, :cols] + terms[:, cols : 2 * cols] + terms[:, 2 * cols :]
        own_ref[...] = jnp.where(named, replaced, blocks[0][...])


def collect(order, unit, chunk, me, pieces, high, low):
    for mask, ref in zip(order, pieces):
        at = pl.ds(pl.multiple_of((me ^ mask) * unit, unit), unit)
        start = 0 if ref.shape[0] == unit else chunk * unit
        high[at, :], low[at, :] = halves(ref[pl.ds(start, unit), :])


def early(order, unit, chunk, *refs):
    *pieces, high, low = refs
    collect(order, unit, chunk, lax.axis_index("pcol"), pieces, high, low)


def solve(fold, order, unit, chunk, top_ref, early_high, early_low, *refs):
    pieces, outs = refs[: len(order)], refs[len(order) :]
    *solved, high, low = outs
    me = lax.axis_index("pcol")
    for mask in range(order[0]):
        at = pl.ds(pl.multiple_of((me ^ mask) * unit, unit), unit)
        high[at, :], low[at, :] = early_high[at, :], early_low[at, :]
    collect(order, unit, chunk, me, pieces, high, low)
    sources = top_ref.shape[0] // (high.shape[0] * (2 if fold else 1))
    row = lax.axis_index("prow")
    first = 1 if fold else 0

    @pl.when((row >= first) & (row < sources))
    def _():
        solved[0][...] = product(high[...], low[...], top_ref[...])

    if fold and chunk == 0:
        half = top_ref.shape[0] // 2

        @pl.when(row == 0)
        def _():
            for i, out in enumerate(solved):
                at = pl.ds(i * half, half)
                out[...] = product(high[:, at], low[:, at], top_ref[pl.ds(0, half), :])


def update(sources, masks, fold, n_cols, own_ref, *refs):
    chunks = 2 if fold else 1
    count = 3 if fold else 1
    solved, refs = refs[:count], refs[count:]
    split, refs = refs[: 2 * chunks], refs[2 * chunks :]
    *got, out_ref, upper = refs
    rows, _ = own_ref.shape
    depth = rows // n_cols
    unit = depth // chunks
    me = lax.axis_index("prow")

    def place(dest, base, chunk, ref):
        for i in range(n_cols):
            at = base + (i * depth + chunk * unit)
            at = at if isinstance(at, int) else pl.multiple_of(at, unit)
            dest[pl.ds(at, unit), :] = ref[pl.ds(i * unit, unit), :]

    @pl.when(me < sources)
    def _():
        place(out_ref, 0, 0, solved[0])

    if fold:
        for source in range(sources):

            @pl.when(me == source)
            def _():
                place(out_ref, 0, 1, solved[1 + source])

    @pl.when(me >= sources)
    def _():
        for m, mask in enumerate(masks):
            source = me ^ mask

            @pl.when(source < sources)
            def _():
                place(upper, pl.multiple_of(source * rows, rows), 0, got[m])

            if fold:
                for s in range(sources):

                    @pl.when(source == s)
                    def _():
                        place(upper, s * rows, 1, got[len(masks) * (1 + s) + m])

        pair = jnp.concatenate(halves(upper[...]), axis=1)
        for chunk in range(chunks):
            part = product(split[2 * chunk][...], split[2 * chunk + 1][...], pair)
            for i in range(n_cols):
                at = pl.ds(i * depth + chunk * unit, unit)
                out_ref[at, :] = own_ref[at, :] - part[i * unit : (i + 1) * unit]


def per_device(matrix, panel, pivots):
    rows, cols = matrix.shape
    block = pivots.shape[0]
    depth = panel.shape[0]
    n_rows, n_cols = lax.axis_size("prow"), lax.axis_size("pcol")
    sources = block // rows
    fold = sources == 2 and depth % 32 == 0
    chunks = 2 if fold else 1
    unit = depth // chunks
    f32, bf16 = jnp.float32, jnp.bfloat16

    if fold:
        *parts, panel = call(
            functools.partial(halve, rows),
            [pltpu.VMEM((unit, block), f32)] * 2 + [pltpu.VMEM((depth, block), f32)],
            [],
            panel,
        )
    else:
        parts = [panel]

    far = []
    for chunk in range(chunks):
        got = [swap(parts[chunk], "pcol", mask) for mask in range(4, n_cols, 2)]
        far.append([piece for block_ in got for piece in (block_, swap(block_, "pcol", 1))])
    near = [panel, swap(panel, "pcol", 2)]
    near = [piece for block_ in near for piece in (block_, swap(block_, "pcol", 1))]
    blocks = [matrix] + [swap(matrix, "prow", mask) for mask in range(1, n_rows)]

    top, own = call(
        functools.partial(prepare, n_rows, sources),
        (pltpu.VMEM((block, 2 * cols), bf16), pltpu.VMEM((rows, cols), f32)),
        [pltpu.VMEM((n_rows * rows, cols), f32)],
        pivots.reshape(1, block), *blocks,
    )

    masks = tuple(range(sources, n_rows))
    solved, split, got = [], [], []
    for chunk in range(chunks):
        terms = [pltpu.VMEM((rows // chunks, block), bf16)] * 2
        high, low = call(functools.partial(early, range(len(near)), unit, chunk), terms, [], *near)
        count = 2 if fold and chunk == 0 else 1
        *pieces, high, low = call(
            functools.partial(solve, fold, tuple(range(len(near), n_cols)), unit, chunk),
            [pltpu.VMEM((rows // chunks, cols), f32)] * count + terms,
            [],
            top, high, low, *far[chunk],
        )
        solved += pieces
        split += [high, low]
    got = [swap(solved[0], "prow", mask) for mask in masks]
    for source, piece in enumerate(solved[1:]):
        got += [swap(piece, "prow", mask, source) for mask in masks]

    return call(
        functools.partial(update, sources, masks, fold, n_cols),
        jax.ShapeDtypeStruct((rows, cols), f32),
        [pltpu.VMEM((block, cols), f32)],
        own, *solved, *split, *got,
    )


def solution(mesh):
    placed = (P("prow", "pcol"), P(("prow", "pcol"), None), P())
    return jax.shard_map(
        per_device, mesh=mesh, in_specs=placed, out_specs=P("prow", "pcol"), check_vma=False
    )
```

```python
import functools

import jax
import jax.numpy as jnp
from jax import lax
from jax.experimental import pallas as pl
from jax.experimental.pallas import tpu as pltpu
from jax.sharding import PartitionSpec as P


VMEM = pl.BlockSpec(memory_space=pltpu.VMEM)


def swap(block, axis, mask):
    return lax.ppermute(block, axis, [(i, i ^ mask) for i in range(lax.axis_size(axis))])


def call(kernel, out_shape, scratch, *args):
    return pl.pallas_call(
        kernel,
        out_shape=out_shape,
        in_specs=[VMEM] * len(args),
        out_specs=jax.tree.map(lambda _: VMEM, out_shape),
        scratch_shapes=scratch,
        compiler_params=pltpu.CompilerParams(vmem_limit_bytes=16 * 2**20),
    )(*(pltpu.with_memory_space_constraint(arg, pltpu.VMEM) for arg in args))


def halves(value):
    high = value.astype(jnp.bfloat16)
    return high, (value - high.astype(jnp.float32)).astype(jnp.bfloat16)


def dot(a, b):
    return lax.dot_general(a, b, (((1,), (0,)), ((), ())), preferred_element_type=jnp.float32)


def product(high, low, pair):
    cols = pair.shape[1] // 2
    both = dot(high, pair)
    return both[:, :cols] + (both[:, cols:] + dot(low, pair[:, :cols]))


def prepare(n_rows, sources, piv_row, *refs):
    *blocks, top_ref, own_ref, whole = refs
    rows, cols = blocks[0].shape
    block = piv_row.shape[1]
    me = lax.axis_index("prow")
    for mask, ref in enumerate(blocks):
        whole[pl.ds(pl.multiple_of((me ^ mask) * rows, rows), rows), :] = ref[...]

    @pl.when(me < sources)
    def _():
        lanes = 128
        pivot = jnp.broadcast_to(piv_row[...], (lanes, block)).T
        high, low = halves(whole[pl.ds(0, block), :])
        picked = jnp.concatenate([high.astype(jnp.float32), low.astype(jnp.float32)], axis=1)
        picked = jnp.where(pivot[:, :1] < block, picked, 0.0)
        for source in range(sources, n_rows):
            ids = lax.broadcasted_iota(jnp.int32, (block, lanes), 1) + source * rows
            chosen = [(pivot - i == ids).astype(jnp.float32).astype(jnp.bfloat16) for i in range(0, rows, lanes)]
            chosen = jnp.concatenate(chosen, axis=1)
            pair = jnp.concatenate(halves(whole[pl.ds(source * rows, rows), :]), axis=1)
            picked = picked + dot(chosen, pair)
        top_ref[...] = picked.astype(jnp.bfloat16)

    @pl.when(me >= sources)
    def _():
        ids = lax.broadcasted_iota(jnp.int32, (rows, block), 0) + me * rows
        match = piv_row[...] == ids
        chosen = match.astype(jnp.float32)
        named = jnp.max(chosen, axis=1, keepdims=True) > 0.0
        old = whole[pl.ds(0, block), :]
        high, middle = halves(old)
        low = (old - high.astype(jnp.float32) - middle.astype(jnp.float32)).astype(jnp.bfloat16)
        terms = dot(chosen.astype(jnp.bfloat16), jnp.concatenate([high, middle, low], axis=1))
        replaced = terms[:, :cols] + terms[:, cols : 2 * cols] + terms[:, 2 * cols :]
        own_ref[...] = jnp.where(named, replaced, blocks[0][...])


def cut(panel_ref, *chunk_refs):
    unit = chunk_refs[0].shape[0]
    for i, ref in enumerate(chunk_refs):
        ref[...] = panel_ref[pl.ds(i * unit, unit), :]


def collect(order, unit, chunk, me, pieces, high, low):
    for mask, ref in zip(order, pieces):
        at = pl.ds(pl.multiple_of((me ^ mask) * unit, unit), unit)
        start = 0 if ref.shape[0] == unit else chunk * unit
        high[at, :], low[at, :] = halves(ref[pl.ds(start, unit), :])


def early(order, unit, chunk, *refs):
    *pieces, high, low = refs
    collect(order, unit, chunk, lax.axis_index("pcol"), pieces, high, low)


def solve(sources, order, unit, chunk, top_ref, early_high, early_low, *refs):
    *pieces, out_ref, high, low = refs
    for mask in range(order[0]):
        at = pl.ds(pl.multiple_of((lax.axis_index("pcol") ^ mask) * unit, unit), unit)
        high[at, :], low[at, :] = early_high[at, :], early_low[at, :]
    collect(order, unit, chunk, lax.axis_index("pcol"), pieces, high, low)

    @pl.when(lax.axis_index("prow") < sources)
    def _():
        out_ref[...] = product(high[...], low[...], top_ref[...])


def update(sources, masks, chunks, n_cols, own_ref, *refs):
    solved, refs = refs[:chunks], refs[chunks:]
    split, refs = refs[: 2 * chunks], refs[2 * chunks :]
    *got, out_ref, upper = refs
    rows, _ = own_ref.shape
    depth = rows // n_cols
    unit = depth // chunks
    me = lax.axis_index("prow")

    @pl.when(me < sources)
    def _():
        for chunk in range(chunks):
            for i in range(n_cols):
                out_ref[pl.ds(i * depth + chunk * unit, unit), :] = solved[chunk][pl.ds(i * unit, unit), :]

    @pl.when(me >= sources)
    def _():
        for m, mask in enumerate(masks):
            source = me ^ mask

            @pl.when(source < sources)
            def _():
                for chunk in range(chunks):
                    ref = got[chunk * len(masks) + m]
                    for i in range(n_cols):
                        at = pl.multiple_of(source * rows, rows) + (i * depth + chunk * unit)
                        upper[pl.ds(pl.multiple_of(at, unit), unit), :] = ref[pl.ds(i * unit, unit), :]

        pair = jnp.concatenate(halves(upper[...]), axis=1)
        for chunk in range(chunks):
            part = product(split[2 * chunk][...], split[2 * chunk + 1][...], pair)
            for i in range(n_cols):
                at = pl.ds(i * depth + chunk * unit, unit)
                out_ref[at, :] = own_ref[at, :] - part[i * unit : (i + 1) * unit]


def per_device(matrix, panel, pivots):
    rows, cols = matrix.shape
    block = pivots.shape[0]
    depth = panel.shape[0]
    n_rows, n_cols = lax.axis_size("prow"), lax.axis_size("pcol")
    sources = block // rows
    chunks = 2 if depth % 32 == 0 else 1
    unit = depth // chunks
    f32, bf16 = jnp.float32, jnp.bfloat16

    parts = [panel]
    if chunks > 1:
        parts = call(cut, [pltpu.VMEM((unit, block), f32)] * chunks, [], panel)

    def both(pieces):
        return [got for piece in pieces for got in (piece, swap(piece, "pcol", 1))]

    near = both([panel, swap(panel, "pcol", 2)])
    far = []
    for chunk in range(chunks):
        pieces = []
        for mask in range(4, n_cols, 4):
            pieces.append(swap(parts[chunk], "pcol", mask))
            pieces.append(swap(pieces[-1], "pcol", 2))
        far.append(both(pieces))
    blocks = [matrix] + [swap(matrix, "prow", mask) for mask in range(1, n_rows)]

    top, own = call(
        functools.partial(prepare, n_rows, sources),
        (pltpu.VMEM((block, 2 * cols), bf16), pltpu.VMEM((rows, cols), f32)),
        [pltpu.VMEM((n_rows * rows, cols), f32)],
        pivots.reshape(1, block), *blocks,
    )

    masks = tuple(range(sources, n_rows))
    solved, split, got = [], [], []
    for chunk in range(chunks):
        terms = [pltpu.VMEM((rows // chunks, block), bf16)] * 2
        high, low = call(functools.partial(early, range(len(near)), unit, chunk), terms, [], *near)
        piece, high, low = call(
            functools.partial(solve, sources, tuple(range(len(near), n_cols)), unit, chunk),
            [pltpu.VMEM((rows // chunks, cols), f32)] + terms,
            [],
            top, high, low, *far[chunk],
        )
        solved.append(piece)
        split += [high, low]
        got += [swap(piece, "prow", mask) for mask in masks]

    return call(
        functools.partial(update, sources, masks, chunks, n_cols),
        jax.ShapeDtypeStruct((rows, cols), f32),
        [pltpu.VMEM((block, cols), f32)],
        own, *solved, *split, *got,
    )


def solution(mesh):
    placed = (P("prow", "pcol"), P(("prow", "pcol"), None), P())
    return jax.shard_map(
        per_device, mesh=mesh, in_specs=placed, out_specs=P("prow", "pcol"), check_vma=False
    )
```

```python
import functools

import jax
import jax.numpy as jnp
from jax import lax
from jax.experimental import pallas as pl
from jax.experimental.pallas import tpu as pltpu
from jax.sharding import PartitionSpec as P


VMEM = pl.BlockSpec(memory_space=pltpu.VMEM)


def swap(block, axis, mask):
    return lax.ppermute(block, axis, [(i, i ^ mask) for i in range(lax.axis_size(axis))])


def call(kernel, out_shape, scratch, *args):
    return pl.pallas_call(
        kernel,
        out_shape=out_shape,
        in_specs=[VMEM] * len(args),
        out_specs=jax.tree.map(lambda _: VMEM, out_shape),
        scratch_shapes=scratch,
        compiler_params=pltpu.CompilerParams(vmem_limit_bytes=16 * 2**20),
    )(*(pltpu.with_memory_space_constraint(arg, pltpu.VMEM) for arg in args))


def halves(value):
    high = value.astype(jnp.bfloat16)
    return high, (value - high.astype(jnp.float32)).astype(jnp.bfloat16)


def dot(a, b):
    return lax.dot_general(a, b, (((1,), (0,)), ((), ())), preferred_element_type=jnp.float32)


def product(high, low, pair):
    cols = pair.shape[1] // 2
    both = dot(high, pair)
    return both[:, :cols] + (both[:, cols:] + dot(low, pair[:, :cols]))


def prepare(n_rows, sources, piv_row, *refs):
    *blocks, top_ref, own_ref, whole = refs
    rows, cols = blocks[0].shape
    block = piv_row.shape[1]
    me = lax.axis_index("prow")
    for mask, ref in enumerate(blocks):
        whole[pl.ds(pl.multiple_of((me ^ mask) * rows, rows), rows), :] = ref[...]

    @pl.when(me < sources)
    def _():
        lanes = 128
        pivot = jnp.broadcast_to(piv_row[...], (lanes, block)).T
        high, low = halves(whole[pl.ds(0, block), :])
        picked = jnp.concatenate([high.astype(jnp.float32), low.astype(jnp.float32)], axis=1)
        picked = jnp.where(pivot[:, :1] < block, picked, 0.0)
        for source in range(sources, n_rows):
            ids = lax.broadcasted_iota(jnp.int32, (block, lanes), 1) + source * rows
            chosen = [(pivot - i == ids).astype(jnp.float32).astype(jnp.bfloat16) for i in range(0, rows, lanes)]
            chosen = jnp.concatenate(chosen, axis=1)
            pair = jnp.concatenate(halves(whole[pl.ds(source * rows, rows), :]), axis=1)
            picked = picked + dot(chosen, pair)
        top_ref[...] = picked.astype(jnp.bfloat16)

    @pl.when(me >= sources)
    def _():
        ids = lax.broadcasted_iota(jnp.int32, (rows, block), 0) + me * rows
        match = piv_row[...] == ids
        chosen = match.astype(jnp.float32)
        named = jnp.max(chosen, axis=1, keepdims=True) > 0.0
        old = whole[pl.ds(0, block), :]
        high, middle = halves(old)
        low = (old - high.astype(jnp.float32) - middle.astype(jnp.float32)).astype(jnp.bfloat16)
        terms = dot(chosen.astype(jnp.bfloat16), jnp.concatenate([high, middle, low], axis=1))
        replaced = terms[:, :cols] + terms[:, cols : 2 * cols] + terms[:, 2 * cols :]
        own_ref[...] = jnp.where(named, replaced, blocks[0][...])


def cut(panel_ref, *chunk_refs):
    unit = chunk_refs[0].shape[0]
    for i, ref in enumerate(chunk_refs):
        ref[...] = panel_ref[pl.ds(i * unit, unit), :]


def collect(pieces, high, low):
    start = 0
    for ref in pieces:
        at = pl.ds(start, ref.shape[0])
        high[at, :], low[at, :] = halves(ref[...])
        start += ref.shape[0]


def early(*refs):
    *pieces, high, low = refs
    collect(pieces, high, low)


def solve(ready, sources, top_ref, *refs):
    *refs, out_ref, high, low = refs
    ready, pieces = refs[: 2 * ready], refs[2 * ready :]
    collect(pieces, high, low)

    @pl.when(lax.axis_index("prow") < sources)
    def _():
        start = 0
        for high_ref, low_ref in (*zip(ready[::2], ready[1::2]), (high, low)):
            at = pl.ds(start, high_ref.shape[0])
            out_ref[at, :] = product(high_ref[...], low_ref[...], top_ref[...])
            start += high_ref.shape[0]


def update(sources, masks, groups, n_split, own_ref, *refs):
    solved, refs = refs[: len(groups)], refs[len(groups) :]
    split, refs = refs[: 2 * n_split], refs[2 * n_split :]
    *got, out_ref, upper = refs
    rows, _ = own_ref.shape
    row, col = lax.axis_index("prow"), lax.axis_index("pcol")
    depth = rows // lax.axis_size("pcol")

    def places(group):
        start = 0
        for mask, first, count in group:
            yield pl.multiple_of((col ^ mask) * depth + first, count), start, count
            start += count

    @pl.when(row < sources)
    def _():
        for group, ref in zip(groups, solved):
            for at, start, count in places(group):
                out_ref[pl.ds(at, count), :] = ref[pl.ds(start, count), :]

    @pl.when(row >= sources)
    def _():
        for m, mask in enumerate(masks):
            source = row ^ mask

            @pl.when(source < sources)
            def _():
                for g, group in enumerate(groups):
                    ref = got[g * len(masks) + m]
                    for at, start, count in places(group):
                        at = pl.multiple_of(source * rows + at, count)
                        upper[pl.ds(at, count), :] = ref[pl.ds(start, count), :]

        pair = jnp.concatenate(halves(upper[...]), axis=1)
        done = jnp.concatenate([product(split[2 * i][...], split[2 * i + 1][...], pair) for i in range(n_split)], axis=0)
        base = 0
        for group in groups:
            for at, start, count in places(group):
                at = pl.ds(at, count)
                out_ref[at, :] = own_ref[at, :] - done[base + start : base + start + count]
            base += sum(count for _, _, count in group)


def per_device(matrix, panel, pivots):
    rows, cols = matrix.shape
    block = pivots.shape[0]
    depth = panel.shape[0]
    n_rows, n_cols = lax.axis_size("prow"), lax.axis_size("pcol")
    sources = block // rows
    chunks = 2 if depth % 32 == 0 else 1
    unit = depth // chunks
    f32, bf16 = jnp.float32, jnp.bfloat16

    parts = [panel]
    if chunks > 1:
        parts = call(cut, [pltpu.VMEM((unit, block), f32)] * chunks, [], panel)

    def both(piece):
        return [piece, swap(piece, "pcol", 1)]

    near = both(panel) + both(swap(panel, "pcol", 2))
    near_at = [(mask, 0, depth) for mask in range(4)]
    far, relayed, far_at, relayed_at = [], [], [], []
    for mask in range(4, n_cols, 4):
        for chunk in range(chunks):
            piece = swap(parts[chunk], "pcol", mask)
            far += both(piece)
            far_at += [(mask, chunk * unit, unit), (mask + 1, chunk * unit, unit)]
            relayed += both(swap(piece, "pcol", 2))
            relayed_at += [(mask + 2, chunk * unit, unit), (mask + 3, chunk * unit, unit)]
    blocks = [matrix] + [swap(matrix, "prow", mask) for mask in range(1, n_rows)]

    top, own = call(
        functools.partial(prepare, n_rows, sources),
        (pltpu.VMEM((block, 2 * cols), bf16), pltpu.VMEM((rows, cols), f32)),
        [pltpu.VMEM((n_rows * rows, cols), f32)],
        pivots.reshape(1, block), *blocks,
    )

    def terms(group):
        return [pltpu.VMEM((sum(count for _, _, count in group), block), bf16)] * 2

    def result(group):
        return [pltpu.VMEM((sum(count for _, _, count in group), cols), f32)]

    groups = (near_at, far_at + relayed_at)
    first, *split0 = call(functools.partial(solve, 0, sources), result(near_at) + terms(near_at), [], top, *near)
    split1 = call(early, terms(far_at), [], *far)
    second, *split2 = call(
        functools.partial(solve, 1, sources), result(groups[1]) + terms(relayed_at), [],
        top, *split1, *relayed,
    )
    masks = tuple(range(sources, n_rows))
    solved = [first, second]
    got = [swap(piece, "prow", mask) for piece in solved for mask in masks]

    return call(
        functools.partial(update, sources, masks, groups, 3),
        jax.ShapeDtypeStruct((rows, cols), f32),
        [pltpu.VMEM((block, cols), f32)],
        own, *solved, *split0, *split1, *split2, *got,
    )


def solution(mesh):
    placed = (P("prow", "pcol"), P(("prow", "pcol"), None), P())
    return jax.shard_map(
        per_device, mesh=mesh, in_specs=placed, out_specs=P("prow", "pcol"), check_vma=False
    )
```

```python
import functools

import jax
import jax.numpy as jnp
from jax import lax
from jax.experimental import pallas as pl
from jax.experimental.pallas import tpu as pltpu
from jax.sharding import PartitionSpec as P


VMEM = pl.BlockSpec(memory_space=pltpu.VMEM)
HBM = pl.BlockSpec(memory_space=pltpu.HBM)


def swap(block, axis, mask):
    return lax.ppermute(block, axis, [(i, i ^ mask) for i in range(lax.axis_size(axis))])


def call(kernel, out_shape, scratch, *args, inside=True):
    return pl.pallas_call(
        kernel,
        out_shape=out_shape,
        in_specs=[VMEM if inside else HBM] * len(args),
        out_specs=jax.tree.map(lambda _: VMEM, out_shape),
        scratch_shapes=scratch,
        compiler_params=pltpu.CompilerParams(vmem_limit_bytes=16 * 2**20),
    )(*(pltpu.with_memory_space_constraint(arg, pltpu.VMEM if inside else pltpu.HBM) for arg in args))


def halves(value):
    high = value.astype(jnp.bfloat16)
    return high, (value - high.astype(jnp.float32)).astype(jnp.bfloat16)


def dot(a, b):
    return lax.dot_general(a, b, (((1,), (0,)), ((), ())), preferred_element_type=jnp.float32)


def product(high, low, pair):
    cols = pair.shape[1] // 2
    both = dot(high, pair)
    return both[:, :cols] + (both[:, cols:] + dot(low, pair[:, :cols]))


def exact(chosen, table):
    cols = table.shape[1]
    high, middle = halves(table)
    low = (table - high.astype(jnp.float32) - middle.astype(jnp.float32)).astype(jnp.bfloat16)
    terms = dot(chosen, jnp.concatenate([high, middle, low], axis=1))
    return terms[:, :cols] + terms[:, cols : 2 * cols] + terms[:, 2 * cols :]


def hot(match):
    return match.astype(jnp.float32).astype(jnp.bfloat16)


def rank(piv_row, sources, rows, slot):
    shape = slot.shape
    first = (lax.broadcasted_iota(jnp.int32, shape, 0) + sources) * rows
    pivot = jnp.broadcast_to(piv_row[...], shape)
    member = (pivot >= first) & (pivot < first + rows)
    count = member.astype(jnp.int32)
    lane = lax.broadcasted_iota(jnp.int32, shape, 1)
    step = 1
    while step < shape[1]:
        count = count + jnp.where(lane >= step, pltpu.roll(count, step, 1), 0)
        step *= 2
    slot[...] = jnp.where(member, count - 1, -1)


def pack(sources, masks, piv_hbm, matrix_hbm, *refs):
    *outs, col_ref, piv_row, matrix_ref, slot, sems = refs
    copies = [
        pltpu.make_async_copy(piv_hbm, piv_row, sems.at[0]),
        pltpu.make_async_copy(matrix_hbm, matrix_ref, sems.at[1]),
    ]
    for copy in copies:
        copy.start()
    for copy in copies:
        copy.wait()
    rows = matrix_ref.shape[0]
    block = piv_row.shape[1]
    cap = outs[0].shape[0]
    me = lax.axis_index("prow")
    rank(piv_row, sources, rows, slot)
    places = lax.broadcasted_iota(jnp.int32, (cap, rows), 0)

    @pl.when(me < sources)
    def _():
        for mask, out in zip(masks, outs):
            mine = slot[pl.ds((me ^ mask) - sources, 1), pl.ds(pl.multiple_of(me * rows, rows), rows)]
            out[...] = exact(hot(places == mine), matrix_ref[...])

    @pl.when(me >= sources)
    def _():
        ids = lax.broadcasted_iota(jnp.int32, (rows, block), 0) + me * rows
        mine = jnp.where(piv_row[...] == ids, slot[pl.ds(me - sources, 1), :], -1)
        col_ref[...] = jnp.broadcast_to(jnp.max(mine, axis=1, keepdims=True), col_ref.shape)
        packed = exact(hot(places == col_ref[...].T[:1, :]), matrix_ref[...])
        for out in outs:
            out[...] = packed


def prepare(sources, masks, piv_row, *refs):
    *refs, top_ref, whole, table, slot = refs
    blocks, packs = refs[:sources], refs[sources:]
    rows = blocks[0].shape[0]
    block = piv_row.shape[1]
    cap = packs[0].shape[0]
    lanes = 128
    me = lax.axis_index("prow")

    @pl.when(me < sources)
    def _():
        table[...] = jnp.zeros_like(table)
        for mask, ref in enumerate(blocks):
            whole[pl.ds(pl.multiple_of((me ^ mask) * rows, rows), rows), :] = ref[...]
        rank(piv_row, sources, rows, slot)
        pivot = jnp.broadcast_to(piv_row[...], (lanes, block)).T
        high, low = halves(whole[...])
        picked = jnp.concatenate([high.astype(jnp.float32), low.astype(jnp.float32)], axis=1)
        picked = jnp.where(pivot[:, :1] < block, picked, 0.0)
        lane = lax.broadcasted_iota(jnp.int32, (block, lanes), 1)
        for mask, ref in zip(masks, packs):
            table[pl.ds(0, cap), :] = ref[...]
            column = jnp.broadcast_to(slot[pl.ds((me ^ mask) - sources, 1), :], (lanes, block)).T
            chosen = [hot(column - i == lane) for i in range(0, table.shape[0], lanes)]
            picked = picked + dot(jnp.concatenate(chosen, axis=1), jnp.concatenate(halves(table[...]), axis=1))
        top_ref[...] = picked.astype(jnp.bfloat16)


def lower(sources, masks, col_ref, matrix_ref, *refs):
    *packs, own_ref, table = refs
    rows, lanes = col_ref.shape
    cap = packs[0].shape[0]
    me = lax.axis_index("prow")

    @pl.when(me >= sources)
    def _():
        table[...] = jnp.zeros_like(table)
        for mask, ref in zip(masks, packs):

            @pl.when((me ^ mask) < sources)
            def _():
                table[pl.ds(0, cap), :] += ref[...]

        column = col_ref[...]
        lane = lax.broadcasted_iota(jnp.int32, (rows, lanes), 1)
        chosen = [hot(column - i == lane) for i in range(0, table.shape[0], lanes)]
        replaced = exact(jnp.concatenate(chosen, axis=1), table[...])
        own_ref[...] = jnp.where(column[:, :1] >= 0, replaced, matrix_ref[...])


def collect(pieces, high, low):
    start = 0
    for ref in pieces:
        at = pl.ds(start, ref.shape[0])
        high[at, :], low[at, :] = halves(ref[...])
        start += ref.shape[0]


def early(*refs):
    *pieces, high, low = refs
    collect(pieces, high, low)


def solve(ready, sources, top_ref, *refs):
    ready, refs = refs[: 2 * ready], refs[2 * ready :]
    out_ref = refs[0]
    split = list(zip(ready[::2], ready[1::2]))
    if len(refs) > 1:
        *pieces, out_ref, high, low = refs
        collect(pieces, high, low)
        split.append((high, low))

    @pl.when(lax.axis_index("prow") < sources)
    def _():
        start = 0
        for high, low in split:
            at = pl.ds(start, high.shape[0])
            out_ref[at, :] = product(high[...], low[...], top_ref[...])
            start += high.shape[0]


def update(sources, masks, groups, n_split, own_ref, *refs):
    solved, refs = refs[: len(groups)], refs[len(groups) :]
    split, refs = refs[: 2 * n_split], refs[2 * n_split :]
    *got, out_ref, upper = refs
    rows, _ = own_ref.shape
    row, col = lax.axis_index("prow"), lax.axis_index("pcol")
    depth = rows // lax.axis_size("pcol")

    def places(group):
        start = 0
        for mask, first, count in group:
            yield pl.multiple_of((col ^ mask) * depth + first, count), start, count
            start += count

    @pl.when(row < sources)
    def _():
        for group, ref in zip(groups, solved):
            for at, start, count in places(group):
                out_ref[pl.ds(at, count), :] = ref[pl.ds(start, count), :]

    @pl.when(row >= sources)
    def _():
        for m, mask in enumerate(masks):
            source = row ^ mask

            @pl.when(source < sources)
            def _():
                for g, group in enumerate(groups):
                    ref = got[g * len(masks) + m]
                    for at, start, count in places(group):
                        at = pl.multiple_of(source * rows + at, count)
                        upper[pl.ds(at, count), :] = ref[pl.ds(start, count), :]

        pair = jnp.concatenate(halves(upper[...]), axis=1)
        done = jnp.concatenate([product(split[2 * i][...], split[2 * i + 1][...], pair) for i in range(n_split)], axis=0)
        base = 0
        for group in groups:
            for at, start, count in places(group):
                at = pl.ds(at, count)
                out_ref[at, :] = own_ref[at, :] - done[base + start : base + start + count]
            base += sum(count for _, _, count in group)


def per_device(matrix, panel, pivots):
    rows, cols = matrix.shape
    block = pivots.shape[0]
    depth = panel.shape[0]
    n_rows, n_cols = lax.axis_size("prow"), lax.axis_size("pcol")
    sources = block // rows
    f32, bf16 = jnp.float32, jnp.bfloat16

    def both(piece):
        return [piece, swap(piece, "pcol", 1)]

    near = both(panel) + both(swap(panel, "pcol", 2))
    first_at = [(mask, 0, depth) for mask in range(4)]
    far, relayed, relayed_at = [], [], []
    for mask in range(4, n_cols, 4):
        piece = swap(panel, "pcol", mask)
        far += both(piece)
        first_at += [(mask, 0, depth), (mask + 1, 0, depth)]
        relayed += both(swap(piece, "pcol", 2))
        relayed_at += [(mask + 2, 0, depth), (mask + 3, 0, depth)]

    lanes = 128
    masks = tuple(range(sources, n_rows))
    below = n_rows - sources
    cap = -(-(block // 2 // below + 8) // 8) * 8
    slot = pltpu.VMEM((-(-below // 8) * 8, block), jnp.int32)
    *packs, column, pivot_row, held = call(
        functools.partial(pack, sources, masks),
        [pltpu.VMEM((cap, cols), f32)] * below
        + [pltpu.VMEM((rows, lanes), jnp.int32), pltpu.VMEM((1, block), jnp.int32), pltpu.VMEM((rows, cols), f32)],
        [slot, pltpu.SemaphoreType.DMA((2,))],
        pivots.reshape(1, block), matrix,
        inside=False,
    )
    blocks = [held] + [swap(matrix, "prow", mask) for mask in range(1, sources)]
    packs = [swap(piece, "prow", mask) for mask, piece in zip(masks, packs)]

    table = pltpu.VMEM((-(-cap // lanes) * lanes, cols), f32)
    top = call(
        functools.partial(prepare, sources, masks),
        pltpu.VMEM((block, 2 * cols), bf16),
        [pltpu.VMEM((block, cols), f32), table, slot],
        pivot_row, *blocks, *packs,
    )
    own = call(
        functools.partial(lower, sources, masks),
        pltpu.VMEM((rows, cols), f32),
        [table],
        column, held, *packs,
    )

    def terms(group):
        return [pltpu.VMEM((sum(count for _, _, count in group), block), bf16)] * 2

    def result(group):
        return pltpu.VMEM((sum(count for _, _, count in group), cols), f32)

    groups = (first_at, relayed_at)
    split0 = call(early, terms(first_at), [], *near, *far)
    first = call(functools.partial(solve, 1, sources), result(first_at), [], top, *split0)
    second, *split1 = call(
        functools.partial(solve, 0, sources), [result(relayed_at)] + terms(relayed_at), [],
        top, *relayed,
    )
    solved = [first, second]
    got = [swap(piece, "prow", mask) for piece in solved for mask in masks]

    return call(
        functools.partial(update, sources, masks, groups, 2),
        jax.ShapeDtypeStruct((rows, cols), f32),
        [pltpu.VMEM((block, cols), f32)],
        own, *solved, *split0, *split1, *got,
    )


def solution(mesh):
    placed = (P("prow", "pcol"), P(("prow", "pcol"), None), P())
    return jax.shard_map(
        per_device, mesh=mesh, in_specs=placed, out_specs=P("prow", "pcol"), check_vma=False
    )
```

```python
import functools

import jax
import jax.numpy as jnp
from jax import lax
from jax.experimental import pallas as pl
from jax.experimental.pallas import tpu as pltpu
from jax.sharding import PartitionSpec as P


VMEM = pl.BlockSpec(memory_space=pltpu.VMEM)
HBM = pl.BlockSpec(memory_space=pltpu.HBM)


def swap(block, axis, mask):
    return lax.ppermute(block, axis, [(i, i ^ mask) for i in range(lax.axis_size(axis))])


def call(kernel, out_shape, scratch, *args, inside=True):
    return pl.pallas_call(
        kernel,
        out_shape=out_shape,
        in_specs=[VMEM if inside else HBM] * len(args),
        out_specs=jax.tree.map(lambda _: VMEM, out_shape),
        scratch_shapes=scratch,
        compiler_params=pltpu.CompilerParams(vmem_limit_bytes=16 * 2**20),
    )(*(pltpu.with_memory_space_constraint(arg, pltpu.VMEM if inside else pltpu.HBM) for arg in args))


def halves(value):
    high = value.astype(jnp.bfloat16)
    return high, (value - high.astype(jnp.float32)).astype(jnp.bfloat16)


def dot(a, b):
    return lax.dot_general(a, b, (((1,), (0,)), ((), ())), preferred_element_type=jnp.float32)


def product(high, low, pair):
    cols = pair.shape[1] // 2
    both = dot(high, pair)
    return both[:, :cols] + (both[:, cols:] + dot(low, pair[:, :cols]))


def exact(chosen, table):
    cols = table.shape[1]
    high, middle = halves(table)
    low = (table - high.astype(jnp.float32) - middle.astype(jnp.float32)).astype(jnp.bfloat16)
    terms = dot(chosen, jnp.concatenate([high, middle, low], axis=1))
    return terms[:, :cols] + terms[:, cols : 2 * cols] + terms[:, 2 * cols :]


def hot(match):
    return match.astype(jnp.float32).astype(jnp.bfloat16)


def rank(piv_row, sources, rows, slot):
    shape = slot.shape
    first = (lax.broadcasted_iota(jnp.int32, shape, 0) + sources) * rows
    pivot = jnp.broadcast_to(piv_row[...], shape)
    member = (pivot >= first) & (pivot < first + rows)
    count = member.astype(jnp.int32)
    lane = lax.broadcasted_iota(jnp.int32, shape, 1)
    step = 1
    while step < shape[1]:
        count = count + jnp.where(lane >= step, pltpu.roll(count, step, 1), 0)
        step *= 2
    slot[...] = jnp.where(member, count - 1, -1)


def pack(sources, masks, piv_hbm, matrix_hbm, *refs):
    *outs, col_ref, piv_row, matrix_ref, slot, sems = refs
    copies = [
        pltpu.make_async_copy(piv_hbm, piv_row, sems.at[0]),
        pltpu.make_async_copy(matrix_hbm, matrix_ref, sems.at[1]),
    ]
    for copy in copies:
        copy.start()
    rows = matrix_ref.shape[0]
    block = piv_row.shape[1]
    cap = outs[0].shape[0]
    me = lax.axis_index("prow")
    copies[0].wait()
    rank(piv_row, sources, rows, slot)

    @pl.when(me >= sources)
    def _():
        ids = lax.broadcasted_iota(jnp.int32, (rows, block), 0) + me * rows
        mine = jnp.where(piv_row[...] == ids, slot[pl.ds(me - sources, 1), :], -1)
        col_ref[...] = jnp.broadcast_to(jnp.max(mine, axis=1, keepdims=True), col_ref.shape)

    copies[1].wait()
    places = lax.broadcasted_iota(jnp.int32, (cap, rows), 0)

    @pl.when(me < sources)
    def _():
        for mask, out in zip(masks, outs):
            mine = slot[pl.ds((me ^ mask) - sources, 1), pl.ds(pl.multiple_of(me * rows, rows), rows)]
            out[...] = exact(hot(places == mine), matrix_ref[...])

    @pl.when(me >= sources)
    def _():
        packed = exact(hot(places == col_ref[...].T[:1, :]), matrix_ref[...])
        for out in outs:
            out[...] = packed


def hots(sources, masks, piv_row, chosen_ref, keep_ref, slot):
    block, lanes = keep_ref.shape
    rows = block // sources
    span = chosen_ref.shape[1] // len(masks)
    me = lax.axis_index("prow")

    @pl.when(me < sources)
    def _():
        rank(piv_row, sources, rows, slot)
        pivot = jnp.broadcast_to(piv_row[...], (lanes, block)).T
        keep_ref[...] = (pivot < block).astype(jnp.float32)
        lane = lax.broadcasted_iota(jnp.int32, (block, lanes), 1)
        for m, mask in enumerate(masks):
            column = jnp.broadcast_to(slot[pl.ds((me ^ mask) - sources, 1), :], (lanes, block)).T
            for i in range(0, span, lanes):
                chosen_ref[:, pl.ds(m * span + i, lanes)] = hot(column - i == lane)


def prepare(sources, masks, chosen_ref, keep_ref, *refs):
    *refs, top_ref, whole, table = refs
    blocks, packs = refs[:sources], refs[sources:]
    rows, cols = blocks[0].shape
    cap = packs[0].shape[0]
    span = table.shape[0] // len(masks)
    me = lax.axis_index("prow")

    @pl.when(me < sources)
    def _():
        for mask, ref in enumerate(blocks):
            whole[pl.ds(pl.multiple_of((me ^ mask) * rows, rows), rows), :] = ref[...]
        for m, ref in enumerate(packs):
            table[pl.ds(m * span, cap), :] = ref[...]
            if span > cap:
                table[pl.ds(m * span + cap, span - cap), :] = jnp.zeros((span - cap, cols), jnp.float32)
        high, low = halves(jnp.where(keep_ref[:, :1] > 0.0, whole[...], 0.0))
        old = jnp.concatenate([high.astype(jnp.float32), low.astype(jnp.float32)], axis=1)
        new = dot(chosen_ref[...], jnp.concatenate(halves(table[...]), axis=1))
        top_ref[...] = (old + new).astype(jnp.bfloat16)


def lower(sources, masks, col_ref, matrix_ref, *refs):
    *packs, own_ref, table = refs
    rows, lanes = col_ref.shape
    cap = packs[0].shape[0]
    me = lax.axis_index("prow")

    @pl.when(me >= sources)
    def _():
        table[...] = jnp.zeros_like(table)
        for mask, ref in zip(masks, packs):

            @pl.when((me ^ mask) < sources)
            def _():
                table[pl.ds(0, cap), :] += ref[...]

        column = col_ref[...]
        lane = lax.broadcasted_iota(jnp.int32, (rows, lanes), 1)
        chosen = [hot(column - i == lane) for i in range(0, table.shape[0], lanes)]
        replaced = exact(jnp.concatenate(chosen, axis=1), table[...])
        own_ref[...] = jnp.where(column[:, :1] >= 0, replaced, matrix_ref[...])


def collect(pieces, high, low):
    start = 0
    for ref in pieces:
        at = pl.ds(start, ref.shape[0])
        high[at, :], low[at, :] = halves(ref[...])
        start += ref.shape[0]


def early(*refs):
    *pieces, high, low = refs
    collect(pieces, high, low)


def solve(ready, sources, top_ref, *refs):
    ready, refs = refs[: 2 * ready], refs[2 * ready :]
    out_ref = refs[0]
    split = list(zip(ready[::2], ready[1::2]))
    if len(refs) > 1:
        *pieces, out_ref, high, low = refs
        collect(pieces, high, low)
        split.append((high, low))

    @pl.when(lax.axis_index("prow") < sources)
    def _():
        start = 0
        for high, low in split:
            at = pl.ds(start, high.shape[0])
            out_ref[at, :] = product(high[...], low[...], top_ref[...])
            start += high.shape[0]


def places(group, col, depth):
    start = 0
    for mask, first, count in group:
        yield pl.multiple_of((col ^ mask) * depth + first, count), start, count
        start += count


def update(sources, masks, groups, later, n_split, own_ref, *refs):
    solved, refs = refs[: len(groups) - later], refs[len(groups) - later :]
    split, refs = refs[: 2 * n_split], refs[2 * n_split :]
    *got, out_ref, upper = refs
    rows = own_ref.shape[0]
    row, col = lax.axis_index("prow"), lax.axis_index("pcol")
    depth = rows // lax.axis_size("pcol")

    @pl.when(row < sources)
    def _():
        for group, ref in zip(groups, solved):
            for at, start, count in places(group, col, depth):
                out_ref[pl.ds(at, count), :] = ref[pl.ds(start, count), :]

    @pl.when(row >= sources)
    def _():
        if later:
            upper[...] = jnp.zeros_like(upper)
        for m, mask in enumerate(masks):
            source = row ^ mask

            @pl.when(source < sources)
            def _():
                for g, group in enumerate(groups[: len(groups) - later]):
                    ref = got[g * len(masks) + m]
                    for at, start, count in places(group, col, depth):
                        at = pl.multiple_of(source * rows + at, count)
                        upper[pl.ds(at, count), :] = ref[pl.ds(start, count), :]

        pair = jnp.concatenate(halves(upper[...]), axis=1)
        done = jnp.concatenate([product(split[2 * i][...], split[2 * i + 1][...], pair) for i in range(n_split)], axis=0)
        base = 0
        for group in groups:
            for at, start, count in places(group, col, depth):
                at = pl.ds(at, count)
                out_ref[at, :] = own_ref[at, :] - done[base + start : base + start + count]
            base += sum(count for _, _, count in group)


def finish(sources, masks, groups, n_split, so_far_ref, solved_ref, *refs):
    split, refs = refs[: 2 * n_split], refs[2 * n_split :]
    *got, out_ref, part = refs
    rows = so_far_ref.shape[0]
    row, col = lax.axis_index("prow"), lax.axis_index("pcol")
    depth = rows // lax.axis_size("pcol")
    last = groups[-1]

    @pl.when(row < sources)
    def _():
        out_ref[...] = so_far_ref[...]
        for at, start, count in places(last, col, depth):
            out_ref[pl.ds(at, count), :] = solved_ref[pl.ds(start, count), :]

    @pl.when(row >= sources)
    def _():
        height = solved_ref.shape[0]
        for m, mask in enumerate(masks):
            source = row ^ mask

            @pl.when(source < sources)
            def _():
                for piece, (distance, _, count) in enumerate(last):
                    at = source * height + (piece // 2 * 2 + ((col ^ distance) & 1)) * count
                    part[pl.ds(pl.multiple_of(at, count), count), :] = got[m][pl.ds(piece * count, count), :]

        total = None
        for source in range(sources):
            for i in range(0, len(last), 2):
                at = pl.multiple_of(source * rows + ((col ^ last[i][0]) // 2) * (2 * depth), 2 * depth)
                at = pl.ds(at, 2 * depth)
                mine = part[pl.ds(source * height + i * depth, 2 * depth), :]
                pair = jnp.concatenate(halves(mine), axis=1)
                done = [product(split[2 * j][:, at], split[2 * j + 1][:, at], pair) for j in range(n_split)]
                done = jnp.concatenate(done, axis=0)
                total = done if total is None else total + done
        base = 0
        for group in groups:
            for at, start, count in places(group, col, depth):
                at = pl.ds(at, count)
                out_ref[at, :] = so_far_ref[at, :] - total[base + start : base + start + count]
            base += sum(count for _, _, count in group)


def per_device(matrix, panel, pivots):
    rows, cols = matrix.shape
    block = pivots.shape[0]
    depth = panel.shape[0]
    n_rows, n_cols = lax.axis_size("prow"), lax.axis_size("pcol")
    sources = block // rows
    f32, bf16 = jnp.float32, jnp.bfloat16

    def both(piece):
        return [piece, swap(piece, "pcol", 1)]

    near = both(panel) + both(swap(panel, "pcol", 2))
    first_at = [(mask, 0, depth) for mask in range(4)]
    far, relayed, relayed_at = [], [], []
    for mask in range(4, n_cols, 4):
        piece = swap(panel, "pcol", mask)
        far += both(piece)
        first_at += [(mask, 0, depth), (mask + 1, 0, depth)]
        relayed += both(swap(piece, "pcol", 2))
        relayed_at += [(mask + 2, 0, depth), (mask + 3, 0, depth)]

    lanes = 128
    masks = tuple(range(sources, n_rows))
    below = n_rows - sources
    cap = -(-(block // 2 // below + 8) // 8) * 8
    slot = pltpu.VMEM((-(-below // 8) * 8, block), jnp.int32)
    *packs, column, pivot_row, held = call(
        functools.partial(pack, sources, masks),
        [pltpu.VMEM((cap, cols), f32)] * below
        + [pltpu.VMEM((rows, lanes), jnp.int32), pltpu.VMEM((1, block), jnp.int32), pltpu.VMEM((rows, cols), f32)],
        [slot, pltpu.SemaphoreType.DMA((2,))],
        pivots.reshape(1, block), matrix,
        inside=False,
    )
    blocks = [held] + [swap(matrix, "prow", mask) for mask in range(1, sources)]
    packs = [swap(piece, "prow", mask) for mask, piece in zip(masks, packs)]

    span = -(-cap // lanes) * lanes
    chosen, keep = call(
        functools.partial(hots, sources, masks),
        [pltpu.VMEM((block, below * span), bf16), pltpu.VMEM((block, lanes), f32)],
        [slot],
        pivot_row,
    )
    top = call(
        functools.partial(prepare, sources, masks),
        pltpu.VMEM((block, 2 * cols), bf16),
        [pltpu.VMEM((block, cols), f32), pltpu.VMEM((below * span, cols), f32)],
        chosen, keep, *blocks, *packs,
    )
    own = call(
        functools.partial(lower, sources, masks),
        pltpu.VMEM((rows, cols), f32),
        [pltpu.VMEM((span, cols), f32)],
        column, held, *packs,
    )

    def terms(group):
        return [pltpu.VMEM((sum(count for _, _, count in group), block), bf16)] * 2

    def result(group):
        return pltpu.VMEM((sum(count for _, _, count in group), cols), f32)

    groups = (first_at, relayed_at)
    split0 = call(early, terms(first_at), [], *near, *far)
    first = call(functools.partial(solve, 1, sources), result(first_at), [], top, *split0)
    second, *split1 = call(
        functools.partial(solve, 0, sources), [result(relayed_at)] + terms(relayed_at), [],
        top, *relayed,
    )
    solved = [first, second]
    got = [swap(piece, "prow", mask) for piece in solved for mask in masks]

    scratch = [pltpu.VMEM((block, cols), f32)]
    if 2 * depth % lanes:
        return call(
            functools.partial(update, sources, masks, groups, 0, 2),
            jax.ShapeDtypeStruct((rows, cols), f32),
            scratch,
            own, *solved, *split0, *split1, *got,
        )
    so_far = call(
        functools.partial(update, sources, masks, groups, 1, 2),
        pltpu.VMEM((rows, cols), f32),
        scratch,
        own, *solved[:-1], *split0, *split1, *got[: -len(masks)],
    )
    return call(
        functools.partial(finish, sources, masks, groups, 2),
        jax.ShapeDtypeStruct((rows, cols), f32),
        [pltpu.VMEM((sources * solved[-1].shape[0], cols), f32)],
        so_far, solved[-1], *split0, *split1, *got[-len(masks) :],
    )


def solution(mesh):
    placed = (P("prow", "pcol"), P(("prow", "pcol"), None), P())
    return jax.shard_map(
        per_device, mesh=mesh, in_specs=placed, out_specs=P("prow", "pcol"), check_vma=False
    )
```

```python
import functools

import jax
import jax.numpy as jnp
from jax import lax
from jax.experimental import pallas as pl
from jax.experimental.pallas import tpu as pltpu
from jax.sharding import PartitionSpec as P


VMEM = pl.BlockSpec(memory_space=pltpu.VMEM)
HBM = pl.BlockSpec(memory_space=pltpu.HBM)


def swap(block, axis, mask):
    return lax.ppermute(block, axis, [(i, i ^ mask) for i in range(lax.axis_size(axis))])


def call(kernel, out_shape, scratch, *args, inside=True):
    return pl.pallas_call(
        kernel,
        out_shape=out_shape,
        in_specs=[VMEM if inside else HBM] * len(args),
        out_specs=jax.tree.map(lambda _: VMEM, out_shape),
        scratch_shapes=scratch,
        compiler_params=pltpu.CompilerParams(vmem_limit_bytes=16 * 2**20),
    )(*(pltpu.with_memory_space_constraint(arg, pltpu.VMEM if inside else pltpu.HBM) for arg in args))


def halves(value):
    high = value.astype(jnp.bfloat16)
    return high, (value - high.astype(jnp.float32)).astype(jnp.bfloat16)


def dot(a, b):
    return lax.dot_general(a, b, (((1,), (0,)), ((), ())), preferred_element_type=jnp.float32)


def product(high, low, pair):
    cols = pair.shape[1] // 2
    both = dot(high, pair)
    return both[:, :cols] + (both[:, cols:] + dot(low, pair[:, :cols]))


def exact(chosen, table):
    cols = table.shape[1]
    high, middle = halves(table)
    low = (table - high.astype(jnp.float32) - middle.astype(jnp.float32)).astype(jnp.bfloat16)
    terms = dot(chosen, jnp.concatenate([high, middle, low], axis=1))
    return terms[:, :cols] + terms[:, cols : 2 * cols] + terms[:, 2 * cols :]


def hot(match):
    return match.astype(jnp.float32).astype(jnp.bfloat16)


def rank(piv_row, sources, rows, slot):
    shape = slot.shape
    first = (lax.broadcasted_iota(jnp.int32, shape, 0) + sources) * rows
    pivot = jnp.broadcast_to(piv_row[...], shape)
    member = (pivot >= first) & (pivot < first + rows)
    count = member.astype(jnp.int32)
    lane = lax.broadcasted_iota(jnp.int32, shape, 1)
    step = 1
    while step < shape[1]:
        count = count + jnp.where(lane >= step, pltpu.roll(count, step, 1), 0)
        step *= 2
    slot[...] = jnp.where(member, count - 1, -1)


def pack(sources, masks, piv_hbm, matrix_hbm, *refs):
    *outs, col_ref, piv_row, matrix_ref, slot, sems = refs
    copies = [
        pltpu.make_async_copy(piv_hbm, piv_row, sems.at[0]),
        pltpu.make_async_copy(matrix_hbm, matrix_ref, sems.at[1]),
    ]
    for copy in copies:
        copy.start()
    rows = matrix_ref.shape[0]
    block = piv_row.shape[1]
    cap = outs[0].shape[0]
    me = lax.axis_index("prow")
    copies[0].wait()
    rank(piv_row, sources, rows, slot)

    @pl.when(me >= sources)
    def _():
        ids = lax.broadcasted_iota(jnp.int32, (rows, block), 0) + me * rows
        mine = jnp.where(piv_row[...] == ids, slot[pl.ds(me - sources, 1), :], -1)
        col_ref[...] = jnp.broadcast_to(jnp.max(mine, axis=1, keepdims=True), col_ref.shape)

    copies[1].wait()
    places = lax.broadcasted_iota(jnp.int32, (cap, rows), 0)

    @pl.when(me < sources)
    def _():
        for mask, out in zip(masks, outs):
            mine = slot[pl.ds((me ^ mask) - sources, 1), pl.ds(pl.multiple_of(me * rows, rows), rows)]
            out[...] = exact(hot(places == mine), matrix_ref[...])

    @pl.when(me >= sources)
    def _():
        packed = exact(hot(places == col_ref[...].T[:1, :]), matrix_ref[...])
        for out in outs:
            out[...] = packed


def hots(sources, masks, piv_row, chosen_ref, keep_ref, slot):
    block, lanes = keep_ref.shape
    rows = block // sources
    span = chosen_ref.shape[1] // len(masks)
    me = lax.axis_index("prow")

    @pl.when(me < sources)
    def _():
        rank(piv_row, sources, rows, slot)
        pivot = jnp.broadcast_to(piv_row[...], (lanes, block)).T
        keep_ref[...] = (pivot < block).astype(jnp.float32)
        lane = lax.broadcasted_iota(jnp.int32, (block, lanes), 1)
        for m, mask in enumerate(masks):
            column = jnp.broadcast_to(slot[pl.ds((me ^ mask) - sources, 1), :], (lanes, block)).T
            for i in range(0, span, lanes):
                chosen_ref[:, pl.ds(m * span + i, lanes)] = hot(column - i == lane)


def prepare(sources, masks, chosen_ref, keep_ref, *refs):
    *refs, top_ref, whole, table = refs
    blocks, packs = refs[:sources], refs[sources:]
    rows, cols = blocks[0].shape
    cap = packs[0].shape[0]
    span = table.shape[0] // len(masks)
    me = lax.axis_index("prow")

    @pl.when(me < sources)
    def _():
        for mask, ref in enumerate(blocks):
            whole[pl.ds(pl.multiple_of((me ^ mask) * rows, rows), rows), :] = ref[...]
        for m, ref in enumerate(packs):
            table[pl.ds(m * span, cap), :] = ref[...]
            if span > cap:
                table[pl.ds(m * span + cap, span - cap), :] = jnp.zeros((span - cap, cols), jnp.float32)
        high, low = halves(jnp.where(keep_ref[:, :1] > 0.0, whole[...], 0.0))
        old = jnp.concatenate([high.astype(jnp.float32), low.astype(jnp.float32)], axis=1)
        new = dot(chosen_ref[...], jnp.concatenate(halves(table[...]), axis=1))
        top_ref[...] = (old + new).astype(jnp.bfloat16)


def lower(sources, masks, col_ref, matrix_ref, *refs):
    *packs, own_ref, table = refs
    rows, lanes = col_ref.shape
    cap = packs[0].shape[0]
    me = lax.axis_index("prow")

    @pl.when(me >= sources)
    def _():
        table[...] = jnp.zeros_like(table)
        for mask, ref in zip(masks, packs):

            @pl.when((me ^ mask) < sources)
            def _():
                table[pl.ds(0, cap), :] += ref[...]

        column = col_ref[...]
        lane = lax.broadcasted_iota(jnp.int32, (rows, lanes), 1)
        chosen = [hot(column - i == lane) for i in range(0, table.shape[0], lanes)]
        replaced = exact(jnp.concatenate(chosen, axis=1), table[...])
        own_ref[...] = jnp.where(column[:, :1] >= 0, replaced, matrix_ref[...])


def collect(pieces, high, low):
    start = 0
    for ref in pieces:
        at = pl.ds(start, ref.shape[0])
        high[at, :], low[at, :] = halves(ref[...])
        start += ref.shape[0]


def early(*refs):
    *pieces, high, low = refs
    collect(pieces, high, low)


def solve(ready, sources, top_ref, *refs):
    ready, refs = refs[: 2 * ready], refs[2 * ready :]
    out_ref = refs[0]
    split = list(zip(ready[::2], ready[1::2]))
    if len(refs) > 1:
        *pieces, out_ref, high, low = refs
        collect(pieces, high, low)
        split.append((high, low))

    @pl.when(lax.axis_index("prow") < sources)
    def _():
        start = 0
        for high, low in split:
            at = pl.ds(start, high.shape[0])
            out_ref[at, :] = product(high[...], low[...], top_ref[...])
            start += high.shape[0]


def places(group, col, depth):
    start = 0
    for mask, first, count in group:
        yield pl.multiple_of((col ^ mask) * depth + first, count), start, count
        start += count


def update(sources, masks, groups, later, n_split, own_ref, *refs):
    solved, refs = refs[: len(groups) - later], refs[len(groups) - later :]
    split, refs = refs[: 2 * n_split], refs[2 * n_split :]
    *got, out_ref, upper = refs
    rows = own_ref.shape[0]
    row, col = lax.axis_index("prow"), lax.axis_index("pcol")
    depth = rows // lax.axis_size("pcol")

    @pl.when(row < sources)
    def _():
        for group, ref in zip(groups, solved):
            for at, start, count in places(group, col, depth):
                out_ref[pl.ds(at, count), :] = ref[pl.ds(start, count), :]

    @pl.when(row >= sources)
    def _():
        if later:
            upper[...] = jnp.zeros_like(upper)
        for m, mask in enumerate(masks):
            source = row ^ mask

            @pl.when(source < sources)
            def _():
                for g, group in enumerate(groups[: len(groups) - later]):
                    ref = got[g * len(masks) + m]
                    for at, start, count in places(group, col, depth):
                        at = pl.multiple_of(source * rows + at, count)
                        upper[pl.ds(at, count), :] = ref[pl.ds(start, count), :]

        pair = jnp.concatenate(halves(upper[...]), axis=1)
        done = jnp.concatenate([product(split[2 * i][...], split[2 * i + 1][...], pair) for i in range(n_split)], axis=0)
        base = 0
        for group in groups:
            for at, start, count in places(group, col, depth):
                at = pl.ds(at, count)
                out_ref[at, :] = own_ref[at, :] - done[base + start : base + start + count]
            base += sum(count for _, _, count in group)


def finish(sources, masks, groups, n_split, so_far_ref, solved_ref, *refs):
    split, refs = refs[: 2 * n_split], refs[2 * n_split :]
    *got, out_ref, part = refs
    rows = so_far_ref.shape[0]
    row, col = lax.axis_index("prow"), lax.axis_index("pcol")
    depth = rows // lax.axis_size("pcol")
    last = groups[-1]

    @pl.when(row < sources)
    def _():
        out_ref[...] = so_far_ref[...]
        for at, start, count in places(last, col, depth):
            out_ref[pl.ds(at, count), :] = solved_ref[pl.ds(start, count), :]

    @pl.when(row >= sources)
    def _():
        height = solved_ref.shape[0]
        for m, mask in enumerate(masks):
            source = row ^ mask

            @pl.when(source < sources)
            def _():
                for piece, (distance, _, count) in enumerate(last):
                    at = source * height + (piece // 2 * 2 + ((col ^ distance) & 1)) * count
                    part[pl.ds(pl.multiple_of(at, count), count), :] = got[m][pl.ds(piece * count, count), :]

        total = None
        for source in range(sources):
            for i in range(0, len(last), 2):
                at = pl.multiple_of(source * rows + ((col ^ last[i][0]) // 2) * (2 * depth), 2 * depth)
                at = pl.ds(at, 2 * depth)
                mine = part[pl.ds(source * height + i * depth, 2 * depth), :]
                pair = jnp.concatenate(halves(mine), axis=1)
                done = [product(split[2 * j][:, at], split[2 * j + 1][:, at], pair) for j in range(n_split)]
                done = jnp.concatenate(done, axis=0)
                total = done if total is None else total + done
        base = 0
        for group in groups:
            for at, start, count in places(group, col, depth):
                at = pl.ds(at, count)
                out_ref[at, :] = so_far_ref[at, :] - total[base + start : base + start + count]
            base += sum(count for _, _, count in group)


def per_device(matrix, panel, pivots):
    rows, cols = matrix.shape
    block = pivots.shape[0]
    depth = panel.shape[0]
    n_rows, n_cols = lax.axis_size("prow"), lax.axis_size("pcol")
    sources = block // rows
    f32, bf16 = jnp.float32, jnp.bfloat16

    def both(piece):
        return [piece, swap(piece, "pcol", 1)]

    near = both(panel) + both(swap(panel, "pcol", 2))
    near_at = [(mask, 0, depth) for mask in range(4)]
    far, far_at, relayed, relayed_at = [], [], [], []
    for mask in range(4, n_cols, 4):
        piece = swap(panel, "pcol", mask)
        far += both(piece)
        far_at += [(mask, 0, depth), (mask + 1, 0, depth)]
        relayed += both(swap(piece, "pcol", 2))
        relayed_at += [(mask + 2, 0, depth), (mask + 3, 0, depth)]

    lanes = 128
    masks = tuple(range(sources, n_rows))
    below = n_rows - sources
    cap = -(-(block // 2 // below + 8) // 8) * 8
    slot = pltpu.VMEM((-(-below // 8) * 8, block), jnp.int32)
    *packs, column, pivot_row, held = call(
        functools.partial(pack, sources, masks),
        [pltpu.VMEM((cap, cols), f32)] * below
        + [pltpu.VMEM((rows, lanes), jnp.int32), pltpu.VMEM((1, block), jnp.int32), pltpu.VMEM((rows, cols), f32)],
        [slot, pltpu.SemaphoreType.DMA((2,))],
        pivots.reshape(1, block), matrix,
        inside=False,
    )
    blocks = [held] + [swap(matrix, "prow", mask) for mask in range(1, sources)]
    packs = [swap(piece, "prow", mask) for mask, piece in zip(masks, packs)]

    span = -(-cap // lanes) * lanes
    chosen, keep = call(
        functools.partial(hots, sources, masks),
        [pltpu.VMEM((block, below * span), bf16), pltpu.VMEM((block, lanes), f32)],
        [slot],
        pivot_row,
    )
    top = call(
        functools.partial(prepare, sources, masks),
        pltpu.VMEM((block, 2 * cols), bf16),
        [pltpu.VMEM((block, cols), f32), pltpu.VMEM((below * span, cols), f32)],
        chosen, keep, *blocks, *packs,
    )
    own = call(
        functools.partial(lower, sources, masks),
        pltpu.VMEM((rows, cols), f32),
        [pltpu.VMEM((span, cols), f32)],
        column, held, *packs,
    )

    def terms(group):
        return [pltpu.VMEM((sum(count for _, _, count in group), block), bf16)] * 2

    def result(group):
        return pltpu.VMEM((sum(count for _, _, count in group), cols), f32)

    groups = (near_at, far_at, relayed_at)
    split0 = call(early, terms(near_at), [], *near)
    first = call(functools.partial(solve, 1, sources), result(near_at), [], top, *split0)
    second, *split1 = call(functools.partial(solve, 0, sources), [result(far_at)] + terms(far_at), [], top, *far)
    third, *split2 = call(
        functools.partial(solve, 0, sources), [result(relayed_at)] + terms(relayed_at), [], top, *relayed
    )
    solved = [first, second, third]
    got = [swap(piece, "prow", mask) for piece in solved for mask in masks]

    scratch = [pltpu.VMEM((block, cols), f32)]
    if 2 * depth % lanes:
        return call(
            functools.partial(update, sources, masks, groups, 0, 3),
            jax.ShapeDtypeStruct((rows, cols), f32),
            scratch,
            own, *solved, *split0, *split1, *split2, *got,
        )
    so_far = call(
        functools.partial(update, sources, masks, groups, 1, 3),
        pltpu.VMEM((rows, cols), f32),
        scratch,
        own, *solved[:-1], *split0, *split1, *split2, *got[: -len(masks)],
    )
    return call(
        functools.partial(finish, sources, masks, groups, 3),
        jax.ShapeDtypeStruct((rows, cols), f32),
        [pltpu.VMEM((sources * solved[-1].shape[0], cols), f32)],
        so_far, solved[-1], *split0, *split1, *split2, *got[-len(masks) :],
    )


def solution(mesh):
    placed = (P("prow", "pcol"), P(("prow", "pcol"), None), P())
    return jax.shard_map(
        per_device, mesh=mesh, in_specs=placed, out_specs=P("prow", "pcol"), check_vma=False
    )
```

```python
import functools

import jax
import jax.numpy as jnp
from jax import lax
from jax.experimental import pallas as pl
from jax.experimental.pallas import tpu as pltpu
from jax.sharding import PartitionSpec as P


VMEM = pl.BlockSpec(memory_space=pltpu.VMEM)
HBM = pl.BlockSpec(memory_space=pltpu.HBM)


def swap(block, axis, mask):
    return lax.ppermute(block, axis, [(i, i ^ mask) for i in range(lax.axis_size(axis))])


def call(kernel, out_shape, scratch, *args, inside=True):
    return pl.pallas_call(
        kernel,
        out_shape=out_shape,
        in_specs=[VMEM if inside else HBM] * len(args),
        out_specs=jax.tree.map(lambda _: VMEM, out_shape),
        scratch_shapes=scratch,
        compiler_params=pltpu.CompilerParams(vmem_limit_bytes=16 * 2**20),
    )(*(pltpu.with_memory_space_constraint(arg, pltpu.VMEM if inside else pltpu.HBM) for arg in args))


def halves(value):
    high = value.astype(jnp.bfloat16)
    return high, (value - high.astype(jnp.float32)).astype(jnp.bfloat16)


def dot(a, b):
    return lax.dot_general(a, b, (((1,), (0,)), ((), ())), preferred_element_type=jnp.float32)


def product(high, low, pair):
    cols = pair.shape[1] // 2
    both = dot(high, pair)
    return both[:, :cols] + (both[:, cols:] + dot(low, pair[:, :cols]))


def exact(chosen, table):
    cols = table.shape[1]
    high, middle = halves(table)
    low = (table - high.astype(jnp.float32) - middle.astype(jnp.float32)).astype(jnp.bfloat16)
    terms = dot(chosen, jnp.concatenate([high, middle, low], axis=1))
    return terms[:, :cols] + terms[:, cols : 2 * cols] + terms[:, 2 * cols :]


def hot(match):
    return match.astype(jnp.float32).astype(jnp.bfloat16)


def rank(piv_row, sources, rows, slot):
    shape = slot.shape
    first = (lax.broadcasted_iota(jnp.int32, shape, 0) + sources) * rows
    pivot = jnp.broadcast_to(piv_row[...], shape)
    member = (pivot >= first) & (pivot < first + rows)
    count = member.astype(jnp.int32)
    lane = lax.broadcasted_iota(jnp.int32, shape, 1)
    step = 1
    while step < shape[1]:
        count = count + jnp.where(lane >= step, pltpu.roll(count, step, 1), 0)
        step *= 2
    slot[...] = jnp.where(member, count - 1, -1)


def pack(sources, masks, piv_hbm, matrix_hbm, *refs):
    *outs, col_ref, piv_row, matrix_ref, slot, sems = refs
    copies = [
        pltpu.make_async_copy(piv_hbm, piv_row, sems.at[0]),
        pltpu.make_async_copy(matrix_hbm, matrix_ref, sems.at[1]),
    ]
    for copy in copies:
        copy.start()
    rows = matrix_ref.shape[0]
    block = piv_row.shape[1]
    cap = outs[0].shape[0]
    me = lax.axis_index("prow")
    copies[0].wait()
    rank(piv_row, sources, rows, slot)

    @pl.when(me >= sources)
    def _():
        ids = lax.broadcasted_iota(jnp.int32, (rows, block), 0) + me * rows
        mine = jnp.where(piv_row[...] == ids, slot[pl.ds(me - sources, 1), :], -1)
        col_ref[...] = jnp.broadcast_to(jnp.max(mine, axis=1, keepdims=True), col_ref.shape)

    copies[1].wait()
    places = lax.broadcasted_iota(jnp.int32, (cap, rows), 0)

    @pl.when(me < sources)
    def _():
        for mask, out in zip(masks, outs):
            mine = slot[pl.ds((me ^ mask) - sources, 1), pl.ds(pl.multiple_of(me * rows, rows), rows)]
            out[...] = exact(hot(places == mine), matrix_ref[...])

    @pl.when(me >= sources)
    def _():
        packed = exact(hot(places == col_ref[...].T[:1, :]), matrix_ref[...])
        for out in outs:
            out[...] = packed


def hots(sources, masks, piv_row, chosen_ref, keep_ref, slot):
    block, lanes = keep_ref.shape
    rows = block // sources
    span = chosen_ref.shape[1] // len(masks)
    me = lax.axis_index("prow")

    @pl.when(me < sources)
    def _():
        rank(piv_row, sources, rows, slot)
        pivot = jnp.broadcast_to(piv_row[...], (lanes, block)).T
        keep_ref[...] = (pivot < block).astype(jnp.float32)
        lane = lax.broadcasted_iota(jnp.int32, (block, lanes), 1)
        for m, mask in enumerate(masks):
            column = jnp.broadcast_to(slot[pl.ds((me ^ mask) - sources, 1), :], (lanes, block)).T
            for i in range(0, span, lanes):
                chosen_ref[:, pl.ds(m * span + i, lanes)] = hot(column - i == lane)


def prepare(sources, masks, chosen_ref, keep_ref, *refs):
    *refs, top_ref, whole, table = refs
    blocks, packs = refs[:sources], refs[sources:]
    rows, cols = blocks[0].shape
    cap = packs[0].shape[0]
    span = table.shape[0] // len(masks)
    me = lax.axis_index("prow")

    @pl.when(me < sources)
    def _():
        for mask, ref in enumerate(blocks):
            whole[pl.ds(pl.multiple_of((me ^ mask) * rows, rows), rows), :] = ref[...]
        for m, ref in enumerate(packs):
            table[pl.ds(m * span, cap), :] = ref[...]
            if span > cap:
                table[pl.ds(m * span + cap, span - cap), :] = jnp.zeros((span - cap, cols), jnp.float32)
        high, low = halves(jnp.where(keep_ref[:, :1] > 0.0, whole[...], 0.0))
        old = jnp.concatenate([high.astype(jnp.float32), low.astype(jnp.float32)], axis=1)
        new = dot(chosen_ref[...], jnp.concatenate(halves(table[...]), axis=1))
        top_ref[...] = (old + new).astype(jnp.bfloat16)


def lower(sources, masks, col_ref, matrix_ref, *refs):
    *packs, own_ref, table = refs
    rows, lanes = col_ref.shape
    cap = packs[0].shape[0]
    me = lax.axis_index("prow")

    @pl.when(me >= sources)
    def _():
        table[...] = jnp.zeros_like(table)
        for mask, ref in zip(masks, packs):

            @pl.when((me ^ mask) < sources)
            def _():
                table[pl.ds(0, cap), :] += ref[...]

        column = col_ref[...]
        lane = lax.broadcasted_iota(jnp.int32, (rows, lanes), 1)
        chosen = [hot(column - i == lane) for i in range(0, table.shape[0], lanes)]
        replaced = exact(jnp.concatenate(chosen, axis=1), table[...])
        own_ref[...] = jnp.where(column[:, :1] >= 0, replaced, matrix_ref[...])


def collect(pieces, high, low):
    start = 0
    for ref in pieces:
        at = pl.ds(start, ref.shape[0])
        high[at, :], low[at, :] = halves(ref[...])
        start += ref.shape[0]


def early(*refs):
    *pieces, high, low = refs
    collect(pieces, high, low)


def solve(ready, sources, top_ref, *refs):
    ready, refs = refs[: 2 * ready], refs[2 * ready :]
    out_ref = refs[0]
    split = list(zip(ready[::2], ready[1::2]))
    if len(refs) > 1:
        *pieces, out_ref, high, low = refs
        collect(pieces, high, low)
        split.append((high, low))

    @pl.when(lax.axis_index("prow") < sources)
    def _():
        start = 0
        for high, low in split:
            at = pl.ds(start, high.shape[0])
            out_ref[at, :] = product(high[...], low[...], top_ref[...])
            start += high.shape[0]


def places(group, col, depth):
    start = 0
    for mask, first, count in group:
        yield pl.multiple_of((col ^ mask) * depth + first, count), start, count
        start += count


def update(sources, masks, groups, later, n_split, own_ref, *refs):
    solved, refs = refs[: len(groups) - later], refs[len(groups) - later :]
    split, refs = refs[: 2 * n_split], refs[2 * n_split :]
    *got, out_ref, upper = refs
    rows = own_ref.shape[0]
    row, col = lax.axis_index("prow"), lax.axis_index("pcol")
    depth = rows // lax.axis_size("pcol")

    @pl.when(row < sources)
    def _():
        for group, ref in zip(groups, solved):
            for at, start, count in places(group, col, depth):
                out_ref[pl.ds(at, count), :] = ref[pl.ds(start, count), :]

    @pl.when(row >= sources)
    def _():
        if later:
            upper[...] = jnp.zeros_like(upper)
        for m, mask in enumerate(masks):
            source = row ^ mask

            @pl.when(source < sources)
            def _():
                for g, group in enumerate(groups[: len(groups) - later]):
                    ref = got[g * len(masks) + m]
                    for at, start, count in places(group, col, depth):
                        at = pl.multiple_of(source * rows + at, count)
                        upper[pl.ds(at, count), :] = ref[pl.ds(start, count), :]

        pair = jnp.concatenate(halves(upper[...]), axis=1)
        done = jnp.concatenate([product(split[2 * i][...], split[2 * i + 1][...], pair) for i in range(n_split)], axis=0)
        base = 0
        for group in groups:
            for at, start, count in places(group, col, depth):
                at = pl.ds(at, count)
                out_ref[at, :] = own_ref[at, :] - done[base + start : base + start + count]
            base += sum(count for _, _, count in group)


def finish(sources, masks, groups, n_split, so_far_ref, solved_ref, *refs):
    split, refs = refs[: 2 * n_split], refs[2 * n_split :]
    *got, out_ref, part = refs
    rows = so_far_ref.shape[0]
    row, col = lax.axis_index("prow"), lax.axis_index("pcol")
    depth = rows // lax.axis_size("pcol")
    last = groups[-1]

    @pl.when(row < sources)
    def _():
        out_ref[...] = so_far_ref[...]
        for at, start, count in places(last, col, depth):
            out_ref[pl.ds(at, count), :] = solved_ref[pl.ds(start, count), :]

    @pl.when(row >= sources)
    def _():
        height = solved_ref.shape[0]
        for m, mask in enumerate(masks):
            source = row ^ mask

            @pl.when(source < sources)
            def _():
                for piece, (distance, _, count) in enumerate(last):
                    at = source * height + (piece // 2 * 2 + ((col ^ distance) & 1)) * count
                    part[pl.ds(pl.multiple_of(at, count), count), :] = got[m][pl.ds(piece * count, count), :]

        total = None
        for source in range(sources):
            for i in range(0, len(last), 2):
                at = pl.multiple_of(source * rows + ((col ^ last[i][0]) // 2) * (2 * depth), 2 * depth)
                at = pl.ds(at, 2 * depth)
                mine = part[pl.ds(source * height + i * depth, 2 * depth), :]
                pair = jnp.concatenate(halves(mine), axis=1)
                done = [product(split[2 * j][:, at], split[2 * j + 1][:, at], pair) for j in range(n_split)]
                done = jnp.concatenate(done, axis=0)
                total = done if total is None else total + done
        base = 0
        for group in groups:
            for at, start, count in places(group, col, depth):
                at = pl.ds(at, count)
                out_ref[at, :] = so_far_ref[at, :] - total[base + start : base + start + count]
            base += sum(count for _, _, count in group)


def per_device(matrix, panel, pivots):
    rows, cols = matrix.shape
    block = pivots.shape[0]
    depth = panel.shape[0]
    n_rows, n_cols = lax.axis_size("prow"), lax.axis_size("pcol")
    sources = block // rows
    f32, bf16 = jnp.float32, jnp.bfloat16

    def both(piece):
        return [piece, swap(piece, "pcol", 1)]

    near = both(panel) + both(swap(panel, "pcol", 2))
    near, far = near[:2], near[2:]
    near_at = [(mask, 0, depth) for mask in range(2)]
    far_at = [(mask, 0, depth) for mask in range(2, 4)]
    relayed, relayed_at = [], []
    for mask in range(4, n_cols, 4):
        piece = swap(panel, "pcol", mask)
        far += both(piece)
        far_at += [(mask, 0, depth), (mask + 1, 0, depth)]
        relayed += both(swap(piece, "pcol", 2))
        relayed_at += [(mask + 2, 0, depth), (mask + 3, 0, depth)]

    lanes = 128
    masks = tuple(range(sources, n_rows))
    below = n_rows - sources
    cap = -(-(block // 2 // below + 8) // 8) * 8
    slot = pltpu.VMEM((-(-below // 8) * 8, block), jnp.int32)
    *packs, column, pivot_row, held = call(
        functools.partial(pack, sources, masks),
        [pltpu.VMEM((cap, cols), f32)] * below
        + [pltpu.VMEM((rows, lanes), jnp.int32), pltpu.VMEM((1, block), jnp.int32), pltpu.VMEM((rows, cols), f32)],
        [slot, pltpu.SemaphoreType.DMA((2,))],
        pivots.reshape(1, block), matrix,
        inside=False,
    )
    blocks = [held] + [swap(matrix, "prow", mask) for mask in range(1, sources)]
    packs = [swap(piece, "prow", mask) for mask, piece in zip(masks, packs)]

    span = -(-cap // lanes) * lanes
    chosen, keep = call(
        functools.partial(hots, sources, masks),
        [pltpu.VMEM((block, below * span), bf16), pltpu.VMEM((block, lanes), f32)],
        [slot],
        pivot_row,
    )
    top = call(
        functools.partial(prepare, sources, masks),
        pltpu.VMEM((block, 2 * cols), bf16),
        [pltpu.VMEM((block, cols), f32), pltpu.VMEM((below * span, cols), f32)],
        chosen, keep, *blocks, *packs,
    )
    own = call(
        functools.partial(lower, sources, masks),
        pltpu.VMEM((rows, cols), f32),
        [pltpu.VMEM((span, cols), f32)],
        column, held, *packs,
    )

    def terms(group):
        return [pltpu.VMEM((sum(count for _, _, count in group), block), bf16)] * 2

    def result(group):
        return pltpu.VMEM((sum(count for _, _, count in group), cols), f32)

    groups = (near_at, far_at, relayed_at)
    split0 = call(early, terms(near_at), [], *near)
    first = call(functools.partial(solve, 1, sources), result(near_at), [], top, *split0)
    second, *split1 = call(functools.partial(solve, 0, sources), [result(far_at)] + terms(far_at), [], top, *far)
    third, *split2 = call(
        functools.partial(solve, 0, sources), [result(relayed_at)] + terms(relayed_at), [], top, *relayed
    )
    solved = [first, second, third]
    got = [swap(piece, "prow", mask) for piece in solved for mask in masks]

    scratch = [pltpu.VMEM((block, cols), f32)]
    if 2 * depth % lanes:
        return call(
            functools.partial(update, sources, masks, groups, 0, 3),
            jax.ShapeDtypeStruct((rows, cols), f32),
            scratch,
            own, *solved, *split0, *split1, *split2, *got,
        )
    so_far = call(
        functools.partial(update, sources, masks, groups, 1, 3),
        pltpu.VMEM((rows, cols), f32),
        scratch,
        own, *solved[:-1], *split0, *split1, *split2, *got[: -len(masks)],
    )
    return call(
        functools.partial(finish, sources, masks, groups, 3),
        jax.ShapeDtypeStruct((rows, cols), f32),
        [pltpu.VMEM((sources * solved[-1].shape[0], cols), f32)],
        so_far, solved[-1], *split0, *split1, *split2, *got[-len(masks) :],
    )


def solution(mesh):
    placed = (P("prow", "pcol"), P(("prow", "pcol"), None), P())
    return jax.shard_map(
        per_device, mesh=mesh, in_specs=placed, out_specs=P("prow", "pcol"), check_vma=False
    )
```

```python
import functools

import jax
import jax.numpy as jnp
from jax import lax
from jax.experimental import pallas as pl
from jax.experimental.pallas import tpu as pltpu
from jax.sharding import PartitionSpec as P


VMEM = pl.BlockSpec(memory_space=pltpu.VMEM)
HBM = pl.BlockSpec(memory_space=pltpu.HBM)


def swap(block, axis, mask):
    return lax.ppermute(block, axis, [(i, i ^ mask) for i in range(lax.axis_size(axis))])


def call(kernel, out_shape, scratch, *args, inside=True):
    return pl.pallas_call(
        kernel,
        out_shape=out_shape,
        in_specs=[VMEM if inside else HBM] * len(args),
        out_specs=jax.tree.map(lambda _: VMEM, out_shape),
        scratch_shapes=scratch,
        compiler_params=pltpu.CompilerParams(vmem_limit_bytes=16 * 2**20),
    )(*(pltpu.with_memory_space_constraint(arg, pltpu.VMEM if inside else pltpu.HBM) for arg in args))


def halves(value):
    high = value.astype(jnp.bfloat16)
    return high, (value - high.astype(jnp.float32)).astype(jnp.bfloat16)


def dot(a, b):
    return lax.dot_general(a, b, (((1,), (0,)), ((), ())), preferred_element_type=jnp.float32)


def product(high, low, pair):
    cols = pair.shape[1] // 2
    both = dot(high, pair)
    return both[:, :cols] + (both[:, cols:] + dot(low, pair[:, :cols]))


def exact(chosen, table):
    cols = table.shape[1]
    high, middle = halves(table)
    low = (table - high.astype(jnp.float32) - middle.astype(jnp.float32)).astype(jnp.bfloat16)
    terms = dot(chosen, jnp.concatenate([high, middle, low], axis=1))
    return terms[:, :cols] + terms[:, cols : 2 * cols] + terms[:, 2 * cols :]


def hot(match):
    return match.astype(jnp.float32).astype(jnp.bfloat16)


def rank(piv_row, sources, rows, slot):
    shape = slot.shape
    first = (lax.broadcasted_iota(jnp.int32, shape, 0) + sources) * rows
    pivot = jnp.broadcast_to(piv_row[...], shape)
    member = (pivot >= first) & (pivot < first + rows)
    count = member.astype(jnp.int32)
    lane = lax.broadcasted_iota(jnp.int32, shape, 1)
    step = 1
    while step < shape[1]:
        count = count + jnp.where(lane >= step, pltpu.roll(count, step, 1), 0)
        step *= 2
    slot[...] = jnp.where(member, count - 1, -1)


def pack(sources, masks, piv_hbm, matrix_hbm, *refs):
    *outs, col_ref, piv_row, matrix_ref, slot, sems = refs
    copies = [
        pltpu.make_async_copy(piv_hbm, piv_row, sems.at[0]),
        pltpu.make_async_copy(matrix_hbm, matrix_ref, sems.at[1]),
    ]
    for copy in copies:
        copy.start()
    rows = matrix_ref.shape[0]
    block = piv_row.shape[1]
    cap = outs[0].shape[0]
    me = lax.axis_index("prow")
    copies[0].wait()
    rank(piv_row, sources, rows, slot)

    @pl.when(me >= sources)
    def _():
        ids = lax.broadcasted_iota(jnp.int32, (rows, block), 0) + me * rows
        mine = jnp.where(piv_row[...] == ids, slot[pl.ds(me - sources, 1), :], -1)
        col_ref[...] = jnp.broadcast_to(jnp.max(mine, axis=1, keepdims=True), col_ref.shape)

    copies[1].wait()
    places = lax.broadcasted_iota(jnp.int32, (cap, rows), 0)

    @pl.when(me < sources)
    def _():
        for mask, out in zip(masks, outs):
            mine = slot[pl.ds((me ^ mask) - sources, 1), pl.ds(pl.multiple_of(me * rows, rows), rows)]
            out[...] = exact(hot(places == mine), matrix_ref[...])

    @pl.when(me >= sources)
    def _():
        packed = exact(hot(places == col_ref[...].T[:1, :]), matrix_ref[...])
        for out in outs:
            out[...] = packed


def hots(sources, masks, piv_row, chosen_ref, keep_ref, slot):
    block, lanes = keep_ref.shape
    rows = block // sources
    span = chosen_ref.shape[1] // len(masks)
    me = lax.axis_index("prow")

    @pl.when(me < sources)
    def _():
        rank(piv_row, sources, rows, slot)
        pivot = jnp.broadcast_to(piv_row[...], (lanes, block)).T
        keep_ref[...] = (pivot < block).astype(jnp.float32)
        lane = lax.broadcasted_iota(jnp.int32, (block, lanes), 1)
        for m, mask in enumerate(masks):
            column = jnp.broadcast_to(slot[pl.ds((me ^ mask) - sources, 1), :], (lanes, block)).T
            for i in range(0, span, lanes):
                chosen_ref[:, pl.ds(m * span + i, lanes)] = hot(column - i == lane)


def prepare(sources, masks, chosen_ref, keep_ref, *refs):
    *refs, top_ref, whole, table = refs
    blocks, packs = refs[:sources], refs[sources:]
    rows, cols = blocks[0].shape
    cap = packs[0].shape[0]
    span = table.shape[0] // len(masks)
    me = lax.axis_index("prow")

    @pl.when(me < sources)
    def _():
        for mask, ref in enumerate(blocks):
            whole[pl.ds(pl.multiple_of((me ^ mask) * rows, rows), rows), :] = ref[...]
        for m, ref in enumerate(packs):
            table[pl.ds(m * span, cap), :] = ref[...]
            if span > cap:
                table[pl.ds(m * span + cap, span - cap), :] = jnp.zeros((span - cap, cols), jnp.float32)
        high, low = halves(jnp.where(keep_ref[:, :1] > 0.0, whole[...], 0.0))
        old = jnp.concatenate([high.astype(jnp.float32), low.astype(jnp.float32)], axis=1)
        new = dot(chosen_ref[...], jnp.concatenate(halves(table[...]), axis=1))
        top_ref[...] = (old + new).astype(jnp.bfloat16)


def lower(sources, masks, col_ref, matrix_ref, *refs):
    *packs, own_ref, table = refs
    rows, lanes = col_ref.shape
    cap = packs[0].shape[0]
    me = lax.axis_index("prow")

    @pl.when(me >= sources)
    def _():
        table[...] = jnp.zeros_like(table)
        for mask, ref in zip(masks, packs):

            @pl.when((me ^ mask) < sources)
            def _():
                table[pl.ds(0, cap), :] += ref[...]

        column = col_ref[...]
        lane = lax.broadcasted_iota(jnp.int32, (rows, lanes), 1)
        chosen = [hot(column - i == lane) for i in range(0, table.shape[0], lanes)]
        replaced = exact(jnp.concatenate(chosen, axis=1), table[...])
        own_ref[...] = jnp.where(column[:, :1] >= 0, replaced, matrix_ref[...])


def collect(pieces, high, low):
    start = 0
    for ref in pieces:
        at = pl.ds(start, ref.shape[0])
        high[at, :], low[at, :] = halves(ref[...])
        start += ref.shape[0]


def early(*refs):
    *pieces, high, low = refs
    collect(pieces, high, low)


def solve(ready, sources, top_ref, *refs):
    ready, refs = refs[: 2 * ready], refs[2 * ready :]
    out_ref = refs[0]
    split = list(zip(ready[::2], ready[1::2]))
    if len(refs) > 1:
        *pieces, out_ref, high, low = refs
        collect(pieces, high, low)
        split.append((high, low))

    @pl.when(lax.axis_index("prow") < sources)
    def _():
        start = 0
        for high, low in split:
            at = pl.ds(start, high.shape[0])
            out_ref[at, :] = product(high[...], low[...], top_ref[...])
            start += high.shape[0]


def places(group, col, depth):
    start = 0
    for mask, first, count in group:
        yield pl.multiple_of((col ^ mask) * depth + first, count), start, count
        start += count


def update(sources, masks, groups, later, n_split, own_ref, *refs):
    solved, refs = refs[: len(groups) - later], refs[len(groups) - later :]
    split, refs = refs[: 2 * n_split], refs[2 * n_split :]
    *got, out_ref, upper = refs
    rows = own_ref.shape[0]
    row, col = lax.axis_index("prow"), lax.axis_index("pcol")
    depth = rows // lax.axis_size("pcol")

    @pl.when(row < sources)
    def _():
        for group, ref in zip(groups, solved):
            for at, start, count in places(group, col, depth):
                out_ref[pl.ds(at, count), :] = ref[pl.ds(start, count), :]

    @pl.when(row >= sources)
    def _():
        if later:
            upper[...] = jnp.zeros_like(upper)
        for m, mask in enumerate(masks):
            source = row ^ mask

            @pl.when(source < sources)
            def _():
                for g, group in enumerate(groups[: len(groups) - later]):
                    ref = got[g * len(masks) + m]
                    for at, start, count in places(group, col, depth):
                        at = pl.multiple_of(source * rows + at, count)
                        upper[pl.ds(at, count), :] = ref[pl.ds(start, count), :]

        pair = jnp.concatenate(halves(upper[...]), axis=1)
        done = jnp.concatenate([product(split[2 * i][...], split[2 * i + 1][...], pair) for i in range(n_split)], axis=0)
        base = 0
        for group in groups:
            for at, start, count in places(group, col, depth):
                at = pl.ds(at, count)
                out_ref[at, :] = own_ref[at, :] - done[base + start : base + start + count]
            base += sum(count for _, _, count in group)


def finish(sources, masks, groups, n_split, so_far_ref, solved_ref, *refs):
    split, refs = refs[: 2 * n_split], refs[2 * n_split :]
    *got, out_ref, part = refs
    rows = so_far_ref.shape[0]
    row, col = lax.axis_index("prow"), lax.axis_index("pcol")
    depth = rows // lax.axis_size("pcol")
    last = groups[-1]

    @pl.when(row < sources)
    def _():
        out_ref[...] = so_far_ref[...]
        for at, start, count in places(last, col, depth):
            out_ref[pl.ds(at, count), :] = solved_ref[pl.ds(start, count), :]

    @pl.when(row >= sources)
    def _():
        height = solved_ref.shape[0]
        for m, mask in enumerate(masks):
            source = row ^ mask

            @pl.when(source < sources)
            def _():
                for piece, (distance, _, count) in enumerate(last):
                    at = source * height + (piece // 2 * 2 + ((col ^ distance) & 1)) * count
                    part[pl.ds(pl.multiple_of(at, count), count), :] = got[m][pl.ds(piece * count, count), :]

        total = None
        for source in range(sources):
            for i in range(0, len(last), 2):
                at = pl.multiple_of(source * rows + ((col ^ last[i][0]) // 2) * (2 * depth), 2 * depth)
                at = pl.ds(at, 2 * depth)
                mine = part[pl.ds(source * height + i * depth, 2 * depth), :]
                pair = jnp.concatenate(halves(mine), axis=1)
                done = [product(split[2 * j][:, at], split[2 * j + 1][:, at], pair) for j in range(n_split)]
                done = jnp.concatenate(done, axis=0)
                total = done if total is None else total + done
        base = 0
        for group in groups:
            for at, start, count in places(group, col, depth):
                at = pl.ds(at, count)
                out_ref[at, :] = so_far_ref[at, :] - total[base + start : base + start + count]
            base += sum(count for _, _, count in group)


def per_device(matrix, panel, pivots):
    rows, cols = matrix.shape
    block = pivots.shape[0]
    depth = panel.shape[0]
    n_rows, n_cols = lax.axis_size("prow"), lax.axis_size("pcol")
    sources = block // rows
    f32, bf16 = jnp.float32, jnp.bfloat16

    def both(piece):
        return [piece, swap(piece, "pcol", 1)]

    near = both(panel) + both(swap(panel, "pcol", 2))
    near, far = near[:2], near[2:]
    near_at = [(mask, 0, depth) for mask in range(2)]
    far_at = [(mask, 0, depth) for mask in range(2, 4)]
    relayed, relayed_at = [], []
    for mask in range(4, n_cols, 4):
        piece = swap(panel, "pcol", mask)
        far += both(piece)
        far_at += [(mask, 0, depth), (mask + 1, 0, depth)]
        relayed += both(swap(piece, "pcol", 2))
        relayed_at += [(mask + 2, 0, depth), (mask + 3, 0, depth)]

    lanes = 128
    masks = tuple(range(sources, n_rows))
    below = n_rows - sources
    cap = -(-(block // 2 // below + 8) // 8) * 8
    slot = pltpu.VMEM((-(-below // 8) * 8, block), jnp.int32)
    *packs, column, pivot_row, held = call(
        functools.partial(pack, sources, masks),
        [pltpu.VMEM((cap, cols), f32)] * below
        + [pltpu.VMEM((rows, lanes), jnp.int32), pltpu.VMEM((1, block), jnp.int32), pltpu.VMEM((rows, cols), f32)],
        [slot, pltpu.SemaphoreType.DMA((2,))],
        pivots.reshape(1, block), matrix,
        inside=False,
    )
    blocks = [held] + [swap(matrix, "prow", mask) for mask in range(1, sources)]
    packs = [swap(piece, "prow", mask) for mask, piece in zip(masks, packs)]

    span = -(-cap // lanes) * lanes
    chosen, keep = call(
        functools.partial(hots, sources, masks),
        [pltpu.VMEM((block, below * span), bf16), pltpu.VMEM((block, lanes), f32)],
        [slot],
        pivot_row,
    )
    top = call(
        functools.partial(prepare, sources, masks),
        pltpu.VMEM((block, 2 * cols), bf16),
        [pltpu.VMEM((block, cols), f32), pltpu.VMEM((below * span, cols), f32)],
        chosen, keep, *blocks, *packs,
    )
    own = call(
        functools.partial(lower, sources, masks),
        pltpu.VMEM((rows, cols), f32),
        [pltpu.VMEM((span, cols), f32)],
        column, held, *packs,
    )

    def terms(group):
        return [pltpu.VMEM((sum(count for _, _, count in group), block), bf16)] * 2

    def result(group):
        return pltpu.VMEM((sum(count for _, _, count in group), cols), f32)

    groups = (near_at, far_at, relayed_at)
    split0 = call(early, terms(near_at), [], *near)
    first = call(functools.partial(solve, 1, sources), result(near_at), [], top, *split0)
    second, *split1 = call(functools.partial(solve, 0, sources), [result(far_at)] + terms(far_at), [], top, *far)
    third, *split2 = call(
        functools.partial(solve, 0, sources), [result(relayed_at)] + terms(relayed_at), [], top, *relayed
    )
    solved = [first, second, third]
    got = []
    for i, piece in enumerate(solved):
        for mask in masks:
            if i == 0 and mask % 2 and mask - 1 in masks:
                got.append(swap(got[-1], "prow", 1))
            else:
                got.append(swap(piece, "prow", mask))

    scratch = [pltpu.VMEM((block, cols), f32)]
    if 2 * depth % lanes:
        return call(
            functools.partial(update, sources, masks, groups, 0, 3),
            jax.ShapeDtypeStruct((rows, cols), f32),
            scratch,
            own, *solved, *split0, *split1, *split2, *got,
        )
    so_far = call(
        functools.partial(update, sources, masks, groups, 1, 3),
        pltpu.VMEM((rows, cols), f32),
        scratch,
        own, *solved[:-1], *split0, *split1, *split2, *got[: -len(masks)],
    )
    return call(
        functools.partial(finish, sources, masks, groups, 3),
        jax.ShapeDtypeStruct((rows, cols), f32),
        [pltpu.VMEM((sources * solved[-1].shape[0], cols), f32)],
        so_far, solved[-1], *split0, *split1, *split2, *got[-len(masks) :],
    )


def solution(mesh):
    placed = (P("prow", "pcol"), P(("prow", "pcol"), None), P())
    return jax.shard_map(
        per_device, mesh=mesh, in_specs=placed, out_specs=P("prow", "pcol"), check_vma=False
    )
```

```python
import functools

import jax
import jax.numpy as jnp
from jax import lax
from jax.experimental import pallas as pl
from jax.experimental.pallas import tpu as pltpu
from jax.sharding import PartitionSpec as P


VMEM = pl.BlockSpec(memory_space=pltpu.VMEM)
HBM = pl.BlockSpec(memory_space=pltpu.HBM)


def swap(block, axis, mask):
    return lax.ppermute(block, axis, [(i, i ^ mask) for i in range(lax.axis_size(axis))])


def call(kernel, out_shape, scratch, *args, inside=True):
    return pl.pallas_call(
        kernel,
        out_shape=out_shape,
        in_specs=[VMEM if inside else HBM] * len(args),
        out_specs=jax.tree.map(lambda _: VMEM, out_shape),
        scratch_shapes=scratch,
        compiler_params=pltpu.CompilerParams(vmem_limit_bytes=16 * 2**20),
    )(*(pltpu.with_memory_space_constraint(arg, pltpu.VMEM if inside else pltpu.HBM) for arg in args))


def halves(value):
    high = value.astype(jnp.bfloat16)
    return high, (value - high.astype(jnp.float32)).astype(jnp.bfloat16)


def dot(a, b):
    return lax.dot_general(a, b, (((1,), (0,)), ((), ())), preferred_element_type=jnp.float32)


def product(high, low, pair):
    cols = pair.shape[1] // 2
    both = dot(high, pair)
    return both[:, :cols] + (both[:, cols:] + dot(low, pair[:, :cols]))


def exact(chosen, table):
    cols = table.shape[1]
    high, middle = halves(table)
    low = (table - high.astype(jnp.float32) - middle.astype(jnp.float32)).astype(jnp.bfloat16)
    terms = dot(chosen, jnp.concatenate([high, middle, low], axis=1))
    return terms[:, :cols] + terms[:, cols : 2 * cols] + terms[:, 2 * cols :]


def hot(match):
    return match.astype(jnp.float32).astype(jnp.bfloat16)


def rank(piv_row, sources, rows, slot):
    shape = slot.shape
    first = (lax.broadcasted_iota(jnp.int32, shape, 0) + sources) * rows
    pivot = jnp.broadcast_to(piv_row[...], shape)
    member = (pivot >= first) & (pivot < first + rows)
    count = member.astype(jnp.int32)
    lane = lax.broadcasted_iota(jnp.int32, shape, 1)
    step = 1
    while step < shape[1]:
        count = count + jnp.where(lane >= step, pltpu.roll(count, step, 1), 0)
        step *= 2
    slot[...] = jnp.where(member, count - 1, -1)


def pack(sources, masks, piv_hbm, matrix_hbm, *refs):
    *outs, col_ref, piv_row, matrix_ref, slot, sems = refs
    copies = [
        pltpu.make_async_copy(piv_hbm, piv_row, sems.at[0]),
        pltpu.make_async_copy(matrix_hbm, matrix_ref, sems.at[1]),
    ]
    for copy in copies:
        copy.start()
    rows = matrix_ref.shape[0]
    block = piv_row.shape[1]
    cap = outs[0].shape[0]
    me = lax.axis_index("prow")
    copies[0].wait()
    rank(piv_row, sources, rows, slot)

    @pl.when(me >= sources)
    def _():
        ids = lax.broadcasted_iota(jnp.int32, (rows, block), 0) + me * rows
        mine = jnp.where(piv_row[...] == ids, slot[pl.ds(me - sources, 1), :], -1)
        col_ref[...] = jnp.broadcast_to(jnp.max(mine, axis=1, keepdims=True), col_ref.shape)

    copies[1].wait()
    places = lax.broadcasted_iota(jnp.int32, (cap, rows), 0)

    @pl.when(me < sources)
    def _():
        for mask, out in zip(masks, outs):
            mine = slot[pl.ds((me ^ mask) - sources, 1), pl.ds(pl.multiple_of(me * rows, rows), rows)]
            out[...] = exact(hot(places == mine), matrix_ref[...])

    @pl.when(me >= sources)
    def _():
        packed = exact(hot(places == col_ref[...].T[:1, :]), matrix_ref[...])
        for out in outs:
            out[...] = packed


def hots(sources, masks, piv_row, chosen_ref, keep_ref, slot):
    block, lanes = keep_ref.shape
    rows = block // sources
    span = chosen_ref.shape[1] // len(masks)
    me = lax.axis_index("prow")

    @pl.when(me < sources)
    def _():
        rank(piv_row, sources, rows, slot)
        pivot = jnp.broadcast_to(piv_row[...], (lanes, block)).T
        keep_ref[...] = (pivot < block).astype(jnp.float32)
        lane = lax.broadcasted_iota(jnp.int32, (block, lanes), 1)
        for m, mask in enumerate(masks):
            column = jnp.broadcast_to(slot[pl.ds((me ^ mask) - sources, 1), :], (lanes, block)).T
            for i in range(0, span, lanes):
                chosen_ref[:, pl.ds(m * span + i, lanes)] = hot(column - i == lane)


def keep(sources, keep_ref, *refs):
    *blocks, old_ref, whole = refs
    rows = blocks[0].shape[0]
    me = lax.axis_index("prow")

    @pl.when(me < sources)
    def _():
        for mask, ref in enumerate(blocks):
            whole[pl.ds(pl.multiple_of((me ^ mask) * rows, rows), rows), :] = ref[...]
        old_ref[...] = jnp.concatenate(halves(jnp.where(keep_ref[:, :1] > 0.0, whole[...], 0.0)), axis=1)


def prepare(sources, masks, chosen_ref, old_ref, *refs):
    *packs, top_ref, table = refs
    cap, cols = packs[0].shape
    span = table.shape[0] // len(masks)

    @pl.when(lax.axis_index("prow") < sources)
    def _():
        for m, ref in enumerate(packs):
            table[pl.ds(m * span, cap), :] = ref[...]
            if span > cap:
                table[pl.ds(m * span + cap, span - cap), :] = jnp.zeros((span - cap, cols), jnp.float32)
        new = dot(chosen_ref[...], jnp.concatenate(halves(table[...]), axis=1))
        top_ref[...] = (old_ref[...].astype(jnp.float32) + new).astype(jnp.bfloat16)


def lower(sources, masks, col_ref, matrix_ref, *refs):
    *packs, own_ref, table = refs
    rows, lanes = col_ref.shape
    cap = packs[0].shape[0]
    me = lax.axis_index("prow")

    @pl.when(me >= sources)
    def _():
        table[...] = jnp.zeros_like(table)
        for mask, ref in zip(masks, packs):

            @pl.when((me ^ mask) < sources)
            def _():
                table[pl.ds(0, cap), :] += ref[...]

        column = col_ref[...]
        lane = lax.broadcasted_iota(jnp.int32, (rows, lanes), 1)
        chosen = [hot(column - i == lane) for i in range(0, table.shape[0], lanes)]
        replaced = exact(jnp.concatenate(chosen, axis=1), table[...])
        own_ref[...] = jnp.where(column[:, :1] >= 0, replaced, matrix_ref[...])


def collect(pieces, high, low):
    start = 0
    for ref in pieces:
        at = pl.ds(start, ref.shape[0])
        high[at, :], low[at, :] = halves(ref[...])
        start += ref.shape[0]


def early(*refs):
    *pieces, high, low = refs
    collect(pieces, high, low)


def solve(ready, sources, top_ref, *refs):
    ready, refs = refs[: 2 * ready], refs[2 * ready :]
    out_ref = refs[0]
    split = list(zip(ready[::2], ready[1::2]))
    if len(refs) > 1:
        *pieces, out_ref, high, low = refs
        collect(pieces, high, low)
        split.append((high, low))

    @pl.when(lax.axis_index("prow") < sources)
    def _():
        start = 0
        for high, low in split:
            at = pl.ds(start, high.shape[0])
            out_ref[at, :] = product(high[...], low[...], top_ref[...])
            start += high.shape[0]


def places(group, col, depth):
    start = 0
    for mask, first, count in group:
        yield pl.multiple_of((col ^ mask) * depth + first, count), start, count
        start += count


def update(sources, masks, groups, later, n_split, own_ref, *refs):
    solved, refs = refs[: len(groups) - later], refs[len(groups) - later :]
    split, refs = refs[: 2 * n_split], refs[2 * n_split :]
    *got, out_ref, upper = refs
    rows = own_ref.shape[0]
    row, col = lax.axis_index("prow"), lax.axis_index("pcol")
    depth = rows // lax.axis_size("pcol")

    @pl.when(row < sources)
    def _():
        for group, ref in zip(groups, solved):
            for at, start, count in places(group, col, depth):
                out_ref[pl.ds(at, count), :] = ref[pl.ds(start, count), :]

    @pl.when(row >= sources)
    def _():
        if later:
            upper[...] = jnp.zeros_like(upper)
        for m, mask in enumerate(masks):
            source = row ^ mask

            @pl.when(source < sources)
            def _():
                for g, group in enumerate(groups[: len(groups) - later]):
                    ref = got[g * len(masks) + m]
                    for at, start, count in places(group, col, depth):
                        at = pl.multiple_of(source * rows + at, count)
                        upper[pl.ds(at, count), :] = ref[pl.ds(start, count), :]

        pair = jnp.concatenate(halves(upper[...]), axis=1)
        done = jnp.concatenate([product(split[2 * i][...], split[2 * i + 1][...], pair) for i in range(n_split)], axis=0)
        base = 0
        for group in groups:
            for at, start, count in places(group, col, depth):
                at = pl.ds(at, count)
                out_ref[at, :] = own_ref[at, :] - done[base + start : base + start + count]
            base += sum(count for _, _, count in group)


def finish(sources, masks, groups, n_split, so_far_ref, solved_ref, *refs):
    split, refs = refs[: 2 * n_split], refs[2 * n_split :]
    *got, out_ref, part = refs
    rows = so_far_ref.shape[0]
    row, col = lax.axis_index("prow"), lax.axis_index("pcol")
    depth = rows // lax.axis_size("pcol")
    last = groups[-1]

    @pl.when(row < sources)
    def _():
        out_ref[...] = so_far_ref[...]
        for at, start, count in places(last, col, depth):
            out_ref[pl.ds(at, count), :] = solved_ref[pl.ds(start, count), :]

    @pl.when(row >= sources)
    def _():
        height = solved_ref.shape[0]
        for m, mask in enumerate(masks):
            source = row ^ mask

            @pl.when(source < sources)
            def _():
                for piece, (distance, _, count) in enumerate(last):
                    at = source * height + (piece // 2 * 2 + ((col ^ distance) & 1)) * count
                    part[pl.ds(pl.multiple_of(at, count), count), :] = got[m][pl.ds(piece * count, count), :]

        total = None
        for source in range(sources):
            for i in range(0, len(last), 2):
                at = pl.multiple_of(source * rows + ((col ^ last[i][0]) // 2) * (2 * depth), 2 * depth)
                at = pl.ds(at, 2 * depth)
                mine = part[pl.ds(source * height + i * depth, 2 * depth), :]
                pair = jnp.concatenate(halves(mine), axis=1)
                done = [product(split[2 * j][:, at], split[2 * j + 1][:, at], pair) for j in range(n_split)]
                done = jnp.concatenate(done, axis=0)
                total = done if total is None else total + done
        base = 0
        for group in groups:
            for at, start, count in places(group, col, depth):
                at = pl.ds(at, count)
                out_ref[at, :] = so_far_ref[at, :] - total[base + start : base + start + count]
            base += sum(count for _, _, count in group)


def per_device(matrix, panel, pivots):
    rows, cols = matrix.shape
    block = pivots.shape[0]
    depth = panel.shape[0]
    n_rows, n_cols = lax.axis_size("prow"), lax.axis_size("pcol")
    sources = block // rows
    f32, bf16 = jnp.float32, jnp.bfloat16

    def both(piece):
        return [piece, swap(piece, "pcol", 1)]

    near = both(panel) + both(swap(panel, "pcol", 2))
    near, far = near[:2], near[2:]
    near_at = [(mask, 0, depth) for mask in range(2)]
    far_at = [(mask, 0, depth) for mask in range(2, 4)]
    relayed, relayed_at = [], []
    for mask in range(4, n_cols, 4):
        piece = swap(panel, "pcol", mask)
        far += both(piece)
        far_at += [(mask, 0, depth), (mask + 1, 0, depth)]
        relayed += both(swap(piece, "pcol", 2))
        relayed_at += [(mask + 2, 0, depth), (mask + 3, 0, depth)]

    lanes = 128
    masks = tuple(range(sources, n_rows))
    below = n_rows - sources
    cap = -(-(block // 2 // below + 8) // 8) * 8
    slot = pltpu.VMEM((-(-below // 8) * 8, block), jnp.int32)
    *packs, column, pivot_row, held = call(
        functools.partial(pack, sources, masks),
        [pltpu.VMEM((cap, cols), f32)] * below
        + [pltpu.VMEM((rows, lanes), jnp.int32), pltpu.VMEM((1, block), jnp.int32), pltpu.VMEM((rows, cols), f32)],
        [slot, pltpu.SemaphoreType.DMA((2,))],
        pivots.reshape(1, block), matrix,
        inside=False,
    )
    blocks = [held] + [swap(matrix, "prow", mask) for mask in range(1, sources)]
    packs = [swap(piece, "prow", mask) for mask, piece in zip(masks, packs)]

    span = -(-cap // lanes) * lanes
    chosen, kept = call(
        functools.partial(hots, sources, masks),
        [pltpu.VMEM((block, below * span), bf16), pltpu.VMEM((block, lanes), f32)],
        [slot],
        pivot_row,
    )
    old = call(
        functools.partial(keep, sources),
        pltpu.VMEM((block, 2 * cols), bf16),
        [pltpu.VMEM((block, cols), f32)],
        kept, *blocks,
    )
    top = call(
        functools.partial(prepare, sources, masks),
        pltpu.VMEM((block, 2 * cols), bf16),
        [pltpu.VMEM((below * span, cols), f32)],
        chosen, old, *packs,
    )
    own = call(
        functools.partial(lower, sources, masks),
        pltpu.VMEM((rows, cols), f32),
        [pltpu.VMEM((span, cols), f32)],
        column, held, *packs,
    )

    def terms(group):
        return [pltpu.VMEM((sum(count for _, _, count in group), block), bf16)] * 2

    def result(group):
        return pltpu.VMEM((sum(count for _, _, count in group), cols), f32)

    groups = (near_at, far_at, relayed_at)
    split0 = call(early, terms(near_at), [], *near)
    first = call(functools.partial(solve, 1, sources), result(near_at), [], top, *split0)
    second, *split1 = call(functools.partial(solve, 0, sources), [result(far_at)] + terms(far_at), [], top, *far)
    third, *split2 = call(
        functools.partial(solve, 0, sources), [result(relayed_at)] + terms(relayed_at), [], top, *relayed
    )
    solved = [first, second, third]
    got = []
    for i, piece in enumerate(solved):
        for mask in masks:
            if i == 0 and mask % 2 and mask - 1 in masks:
                got.append(swap(got[-1], "prow", 1))
            else:
                got.append(swap(piece, "prow", mask))

    scratch = [pltpu.VMEM((block, cols), f32)]
    if 2 * depth % lanes:
        return call(
            functools.partial(update, sources, masks, groups, 0, 3),
            jax.ShapeDtypeStruct((rows, cols), f32),
            scratch,
            own, *solved, *split0, *split1, *split2, *got,
        )
    so_far = call(
        functools.partial(update, sources, masks, groups, 1, 3),
        pltpu.VMEM((rows, cols), f32),
        scratch,
        own, *solved[:-1], *split0, *split1, *split2, *got[: -len(masks)],
    )
    return call(
        functools.partial(finish, sources, masks, groups, 3),
        jax.ShapeDtypeStruct((rows, cols), f32),
        [pltpu.VMEM((sources * solved[-1].shape[0], cols), f32)],
        so_far, solved[-1], *split0, *split1, *split2, *got[-len(masks) :],
    )


def solution(mesh):
    placed = (P("prow", "pcol"), P(("prow", "pcol"), None), P())
    return jax.shard_map(
        per_device, mesh=mesh, in_specs=placed, out_specs=P("prow", "pcol"), check_vma=False
    )
```
